32 devices in a mesh: groups: 2 (over y), frame: 4 (over z), patch: 2 (over x), head: 2 (over core).
Axes of the slice: x: 2, y: 2, z: 4, core: 2. Of those that a mesh axis runs over, the one named last changes fastest.
Arguments:
- video: bfloat16 [16, 8, 1152], P(('groups', 'frame'), 'patch'), parts along dimension 0, may hold values from -1.5 to 1.5
- gain_time: float32 [1152], replicated, may hold values from 0.1 to 1.9
- qkv_time: bfloat16 [1152, 3, 1152], P('frame', None, 'head'), may hold values from -0.5343196 to 0.5343196
- out_time: bfloat16 [1152, 1152], P('frame', 'head'), may hold values from -0.1875 to 0.1875
- gain_space: float32 [1152], replicated, may hold values from 0.1 to 1.9
- qkv_space: bfloat16 [1152, 3, 1152], P('frame', None, 'head'), may hold values from -0.5343196 to 0.5343196
- out_space: bfloat16 [1152, 1152], P('frame', 'head'), may hold values from -0.1875 to 0.1875
Outputs:
- result: float32 [16, 8, 1152], P(('groups', 'frame', 'patch')), parts along dimension 0
The draws below stay inside these ranges and needn't reach their ends.
There are 2 independent parts, one for each index of `groups`. The reference program is written for one: setup_inputs(seed, part) draws one part's arguments, and reference() takes and returns one part's arrays. A program takes and returns all parts, laid end to end along the dimension named above; an argument that names none is the same for every part. Nothing has to cross between parts.
All inputs are finite; a program needn't handle non-finite values.
Results may differ from the reference program's by a relative error of at most 0.04.
Values may be sent and summed in bfloat16 or wider, within the bound.
No kernel may reach another device: no remote copies, remote signals or barrier semaphores. Data moves between devices by JAX's collectives and lax.ppermute only.
A program may use at most 64 MiB of HBM per device.

```python
import jax
import jax.numpy as jnp
from jax import lax

D = 1152
HEADS = 16
HEAD_WIDTH = 72
FRAMES = 8
PATCHES = 8
N_HEAD = 2


def draw_video(key, part):
    value_rows = 0.25 * jnp.clip(jax.random.normal(jax.random.fold_in(key, 7), (FRAMES, PATCHES, D), jnp.float32), -6.0, 6.0)
    return value_rows.astype(jnp.bfloat16)


def drawn_weight(key):
    matrix_key = jax.random.fold_in(key, 1)
    matrix = jnp.clip(jax.random.normal(matrix_key, (D, 3, D), jnp.float32), -3.0, 3.0) * (1.0 / D ** 0.5)
    return matrix.astype(jnp.bfloat16)


def draw_qkv_time(key, part):
    return drawn_weight(jax.random.fold_in(key, 21))


def draw_qkv_space(key, part):
    return drawn_weight(jax.random.fold_in(key, 37))


def levels(key, extent, cuts, smallest, largest):
    def one(dim, parts):
        draws = jax.random.uniform(jax.random.fold_in(jax.random.fold_in(key, 6), dim), (parts,), jnp.float32, smallest / len(cuts), largest / len(cuts))
        return jnp.repeat(jnp.exp(draws), extent[dim] // parts).reshape((-1,) + (1,) * (len(extent) - dim - 1))

    factor_of = one(*cuts[0])
    for cut in cuts[1:]:
        factor_of = factor_of * one(*cut)
    return factor_of


def scatter_about(own_key, extent, scale, bound, pieces=(), kind=jnp.bfloat16):
    factor_of = levels(own_key, extent, pieces, -0.22, 0.18) if pieces else 1.0
    array = jax.random.normal(own_key, extent, jnp.float32) * scale * factor_of
    return jnp.minimum(jnp.maximum(array, -bound), bound).astype(kind)


def setup_inputs(seed: int = 0, part: int = 0) -> dict:
    key_of = jax.random.split(jax.random.key(seed), 8)
    part_keys = jax.random.split(jax.random.fold_in(key_of[7], part), 8)
    return {
        "video": draw_video(jax.random.fold_in(jax.random.fold_in(key_of[7], part), 71), part),
        "gain_time": jnp.clip(1.0 + 0.18 * jax.random.normal(key_of[1], (D,), jnp.float32), 0.1, 1.9),
        "qkv_time": draw_qkv_time(jax.random.fold_in(key_of[7], 71), part),
        "out_time": scatter_about(key_of[3], (D, D), D ** -0.5, 0.1875, ((0, 4), (1, 2))),
        "gain_space": jnp.clip(1.0 + 0.18 * jax.random.normal(key_of[4], (D,), jnp.float32), 0.1, 1.9),
        "qkv_space": draw_qkv_space(jax.random.fold_in(key_of[7], 71), part),
        "out_space": scatter_about(key_of[6], (D, D), D ** -0.5, 0.1875, ((0, 4), (1, 2))),
    }


def layer_norm(tokens, gain):
    value_rows = tokens.astype(jnp.float32)
    center = lax.optimization_barrier(jnp.mean(value_rows, axis=-1, keepdims=True))
    spread = lax.optimization_barrier(jnp.mean((value_rows - center) ** 2, axis=-1, keepdims=True))
    return ((value_rows - center) * lax.rsqrt(spread + 1e-06) * gain).astype(jnp.bfloat16)

def attend_one(packed):
    query_rows = packed[:, 0].astype(jnp.float32)
    key_rows = packed[:, 1].astype(jnp.float32)
    value_rows = packed[:, 2].astype(jnp.float32)
    score_matrix = jnp.einsum('pzo,ezo->zpe', query_rows, key_rows) / jnp.sqrt(jnp.float32(HEAD_WIDTH))
    attention_weights = jax.nn.softmax(score_matrix, axis=-1).astype(jnp.bfloat16).astype(jnp.float32)
    attention_output = jnp.einsum('jrc,cjn->rjn', attention_weights, value_rows).astype(jnp.bfloat16)
    return attention_output.reshape(attention_output.shape[0], -1)

def mix_block(tokens, gain, qkv_weight, out_weight, over_first):
    rows_a, rows_b, width = tokens.shape
    flat = tokens.reshape(rows_a * rows_b, width)
    normed = layer_norm(flat, gain)
    qkv = jnp.dot(normed, qkv_weight.reshape(width, 3 * width), preferred_element_type=jnp.float32)
    qkv = qkv.astype(jnp.bfloat16).reshape(rows_a, rows_b, 3, HEADS, HEAD_WIDTH)
    if over_first:
        batches = jnp.transpose(qkv, (1, 0, 2, 3, 4))
        attended = jnp.transpose(lax.map(attend_one, batches), (1, 0, 2))
    else:
        attended = lax.map(attend_one, qkv)
    attended = attended.reshape(rows_a * rows_b, width)
    share = width // N_HEAD
    total = jnp.zeros((rows_a * rows_b, width), jnp.float32)
    for group in range(N_HEAD):
        partial_value = jnp.dot(attended[:, group * share:(group + 1) * share], out_weight[:, group * share:(group + 1) * share].T, preferred_element_type=jnp.float32)
        total = total + lax.optimization_barrier(partial_value.astype(jnp.bfloat16)).astype(jnp.float32)
    return (flat.astype(jnp.float32) + total).reshape(rows_a, rows_b, width)

def reference(video, gain_time, qkv_time, out_time, gain_space, qkv_space, out_space):
    after_time = mix_block(video, gain_time, qkv_time, out_time, True).astype(jnp.bfloat16)
    return mix_block(after_time, gain_space, qkv_space, out_space, False)
```

```python
import functools

import jax
import jax.numpy as jnp
from jax import lax
from jax.experimental import pallas as pl
from jax.experimental.pallas import tpu as pltpu
from jax.sharding import PartitionSpec as P

HEAD_WIDTH = 72


def layer_norm(tokens, gain):
    value_rows = tokens.astype(jnp.float32)
    center = jnp.mean(value_rows, axis=-1, keepdims=True)
    spread = jnp.mean((value_rows - center) ** 2, axis=-1, keepdims=True)
    return ((value_rows - center) * lax.rsqrt(spread + 1e-06) * gain).astype(jnp.bfloat16)


def project_qkv(normed, weight):
    columns = weight.shape[1] * weight.shape[2]
    total = jnp.dot(
        normed, weight.reshape(weight.shape[0], columns), preferred_element_type=jnp.float32
    )
    return total.astype(jnp.bfloat16)


def project_out(attended, weight):
    return lax.dot_general(
        attended, weight, (((1,), (1,)), ((), ())), preferred_element_type=jnp.float32
    )


def attend(qkv, over_first):
    query_rows, key_rows, value_rows = (qkv[:, :, 0], qkv[:, :, 1], qkv[:, :, 2])
    factor = 1.0 / jnp.sqrt(jnp.float32(HEAD_WIDTH))
    if over_first:
        score_matrix = (
            jnp.einsum("abhd,cbhd->bhac", query_rows, key_rows, preferred_element_type=jnp.float32)
            * factor
        )
        attention_weights = jax.nn.softmax(score_matrix, axis=-1).astype(jnp.bfloat16)
        attention_output = jnp.einsum(
            "bhac,cbhd->abhd", attention_weights, value_rows, preferred_element_type=jnp.float32
        )
    else:
        score_matrix = (
            jnp.einsum("abhd,achd->ahbc", query_rows, key_rows, preferred_element_type=jnp.float32)
            * factor
        )
        attention_weights = jax.nn.softmax(score_matrix, axis=-1).astype(jnp.bfloat16)
        attention_output = jnp.einsum(
            "ahbc,achd->abhd", attention_weights, value_rows, preferred_element_type=jnp.float32
        )
    return attention_output.astype(jnp.bfloat16)


def mix_partial(tokens, gain, qkv_weight, out_weight, over_first):
    rows_a, rows_b, width = tokens.shape
    flat = tokens.reshape(rows_a * rows_b, width)
    normed = layer_norm(flat, gain)
    qkv = project_qkv(normed, qkv_weight).reshape(rows_a, rows_b, 3, -1, HEAD_WIDTH)
    attended = attend(qkv, over_first).reshape(rows_a * rows_b, -1)
    partial_value = project_out(attended, out_weight)
    rounded = lax.optimization_barrier(partial_value.astype(jnp.bfloat16)).astype(jnp.float32)
    return (flat, rounded)


def on_device(video, gain_time, qkv_time, out_time, gain_space, qkv_space, out_space):
    frame_size = lax.axis_size("frame")
    patch_size = lax.axis_size("patch")
    device_count = frame_size * patch_size
    series = lax.all_to_all(video, "frame", split_axis=1, concat_axis=0, tiled=True)
    qkv_time, out_time, qkv_space, out_space = (
        lax.all_gather(qkv_time, "frame", axis=0, tiled=True),
        lax.all_gather(out_time, "frame", axis=0, tiled=True),
        lax.all_gather(qkv_space, "frame", axis=0, tiled=True),
        lax.all_gather(out_space, "frame", axis=0, tiled=True),
    )
    frame_count, series_count, width = series.shape
    set_count = frame_count // device_count
    flat, rounded = mix_partial(series, gain_time, qkv_time, out_time, True)
    summed = (
        lax.psum(rounded.astype(jnp.bfloat16), "head")
        .astype(jnp.float32)
        .reshape(device_count, set_count, series_count, width)
    )
    resident = flat.reshape(device_count, set_count, series_count, width)
    after_time = (resident.astype(jnp.float32) + summed).astype(jnp.bfloat16)
    arrived = lax.all_to_all(
        after_time, ("frame", "patch"), split_axis=0, concat_axis=2, tiled=True
    )
    whole_frames = arrived.reshape(set_count, device_count * series_count, width)
    whole_frames = whole_frames.reshape(set_count, frame_size, patch_size, series_count, width)
    whole_frames = jnp.transpose(whole_frames, (0, 2, 1, 3, 4)).reshape(
        set_count, device_count * series_count, width
    )
    flat_space, rounded_space = mix_partial(whole_frames, gain_space, qkv_space, out_space, False)
    summed_space = lax.psum(rounded_space.astype(jnp.bfloat16), "head").astype(jnp.float32)
    result = flat_space.astype(jnp.float32) + summed_space
    return result.reshape(whole_frames.shape)


F32 = jnp.float32
BF16 = jnp.bfloat16
KINDS = 3
NT = (((1,), (1,)), ((), ()))


def run(body, outs, *args, scratch=()):
    vmem = pl.BlockSpec(memory_space=pltpu.VMEM)
    single = not isinstance(outs, list)
    shapes = [jax.ShapeDtypeStruct(*o) for o in ([outs] if single else outs)]
    found = pl.pallas_call(
        body,
        out_shape=shapes,
        in_specs=[vmem] * len(args),
        out_specs=[vmem] * len(shapes),
        scratch_shapes=[pltpu.VMEM(*s) for s in scratch],
    )(*args)
    return found[0] if single else found


def lanes(value, start, size):
    return lax.slice_in_dim(value, start, start + size, axis=1)


def exchange(messages):
    count = len(messages)
    return [messages[0]] + [
        lax.ppermute(messages[k], "frame", [(i, i ^ k) for i in range(count)])
        for k in range(1, count)
    ]


def pick_rows(value, source):
    column = lax.broadcasted_iota(jnp.int32, (source.shape[0], value.shape[0]), 1)
    chosen = jnp.where(column == source, 1.0, 0.0).astype(BF16)
    return jnp.dot(chosen, value.astype(BF16), preferred_element_type=F32)


def split_body(count, video_ref, gain_ref, *refs):
    outs, held = refs[:count], refs[count]
    f = lax.axis_index("frame")
    rows = video_ref.shape[0] * video_ref.shape[1]
    share = held.shape[2]
    x = jnp.concatenate([video_ref[i].astype(F32) for i in range(video_ref.shape[0])], axis=0)
    mean = jnp.mean(x, axis=-1, keepdims=True)
    centred = x - mean
    spread = jnp.mean(centred * centred, axis=-1, keepdims=True)
    y = centred * lax.rsqrt(spread + 1e-06) * gain_ref[...]
    for s in range(count):
        held[s, 0:rows] = lanes(y, s * share, share)
        held[s, rows:] = lanes(x, s * share, share)
    for k in range(count):
        outs[k][...] = held[f ^ k].astype(BF16)


def project_body(count, *refs):
    parts, weight_ref, outs = refs[:count], refs[count], refs[count + 1 : 2 * count + 1]
    tokens, total = refs[2 * count + 1 :]
    f = lax.axis_index("frame")
    rows = tokens.shape[0] // count
    for k in range(count):
        place = pl.multiple_of((f ^ k) * rows, rows)
        tokens[pl.ds(place, rows), :] = parts[k][0:rows].astype(F32)
    row = lax.broadcasted_iota(jnp.int32, (tokens.shape[0], 1), 0)
    source = lax.rem(row, rows) * count + lax.div(row, rows)
    x = pick_rows(tokens[...], source).astype(BF16)
    for t in range(KINDS):
        total[t] = jnp.dot(x, weight_ref[t], preferred_element_type=F32)
    for k in range(count):
        place = pl.multiple_of((f ^ k) * rows, rows)
        for t in range(KINDS):
            outs[k][t] = total.at[t][pl.ds(place, rows), :].astype(BF16)


def prepare_body(count, *refs):
    parts, gain_ref, weight_ref = refs[:count], refs[count], refs[count + 1]
    fixed_ref, gain_own, raw_own, raw_other, gains, raw = refs[count + 2 :]
    f, p = lax.axis_index("frame"), lax.axis_index("patch")
    share = gains.shape[2]
    for s in range(count):
        gains[s] = jnp.broadcast_to(lanes(gain_ref[...], s * share, share), gains.shape[1:])
    g = gains[f]
    gain_own[...] = g
    g = g.astype(BF16)
    rows = [jnp.dot(g, weight_ref[t], preferred_element_type=F32) for t in range(KINDS)]
    row = lax.broadcasted_iota(jnp.int32, rows[0].shape, 0)
    fixed_ref[...] = jnp.where(row == 0, rows[0], jnp.where(row == 1, rows[1], rows[2]))
    whole = parts[0].shape[0] // 2
    places = whole // 2
    for k in range(count):
        raw[f ^ k] = parts[k][whole:].astype(F32)
    even, odd = (
        jnp.concatenate([raw[s][at : at + places] for s in range(count)], axis=0)
        for at in (0, places)
    )
    raw_own[...] = jnp.where(p == 0, even, odd).astype(BF16)
    raw_other[...] = jnp.where(p == 0, odd, even).astype(BF16)


def attend_rows(query, key, value):
    rows, width = query.shape
    heads = width // HEAD_WIDTH
    spread = heads * rows
    first = lax.broadcasted_iota(jnp.int32, (heads, rows, width), 0) * HEAD_WIDTH
    first = first.reshape(spread, width)
    lane = lax.broadcasted_iota(jnp.int32, (spread, width), 1)
    mine = (lane >= first) & (lane < first + HEAD_WIDTH)
    keys = jnp.where(mine, jnp.concatenate([key] * heads, axis=0), 0.0).astype(BF16)
    values = jnp.where(mine, jnp.concatenate([value] * heads, axis=0), 0.0).astype(BF16)
    scores = lax.dot_general(keys, query.astype(BF16), NT, preferred_element_type=F32)
    scores = (scores * (1.0 / HEAD_WIDTH**0.5)).reshape(heads, rows, rows)
    power = jnp.exp(scores - jnp.max(scores, axis=1, keepdims=True))
    weights = power / jnp.sum(power, axis=1, keepdims=True)
    weights = weights.reshape(spread, rows).T.astype(BF16)
    return jnp.dot(weights, values, preferred_element_type=F32)


def attend_time_body(count, *refs):
    parts, fixed_ref, out_ref = refs[:count], refs[count], refs[count + 1]
    qkv = []
    for t in range(KINDS):
        total = parts[0][t].astype(F32)
        for k in range(1, count):
            total = total + parts[k][t].astype(F32)
        qkv.append(total.astype(BF16).astype(F32))
    attended = attend_rows(*qkv)
    out_ref[...] = jnp.concatenate([attended, fixed_ref[...]], axis=0).astype(BF16)


def out_time_body(count, *refs):
    parts, weight_ref, raw_other = refs[:count], refs[count], refs[count + 1]
    own_ref, other_ref, tokens = refs[count + 2 :]
    f, p = lax.axis_index("frame"), lax.axis_index("patch")
    rows = tokens.shape[0] // count
    for k in range(count):
        place = pl.multiple_of((f ^ k) * rows, rows)
        tokens[pl.ds(place, rows), :] = parts[k][0:rows].astype(F32)
    half = tokens.shape[0] // 2
    row = lax.broadcasted_iota(jnp.int32, (tokens.shape[0], 1), 0)
    parity = jnp.where(row < half, p, 1 - p)
    row = lax.rem(row, half)
    source = lax.rem(row, count) * rows + 2 * lax.div(row, count) + parity
    x = pick_rows(tokens[...], source).astype(BF16)
    total = lax.dot_general(x, weight_ref[...], NT, preferred_element_type=F32)
    own_ref[...] = total[0:half].astype(BF16)
    other_ref[0:half] = total[half:].astype(BF16)
    other_ref[half:] = raw_other[...]


def in_three(value):
    high = value.astype(BF16).astype(F32)
    middle = (value - high).astype(BF16).astype(F32)
    return high, middle, value - high - middle


def project_space_body(count, *refs):
    own, own_head, cross, cross_head, raw_own, gain_ref, weight_ref = refs[:7]
    outs, after_ref, total = refs[7 : 7 + count], *refs[7 + count :]
    f, p = lax.axis_index("frame"), lax.axis_index("patch")
    half = own.shape[0]
    summed = own[...].astype(F32) + own_head[...].astype(F32)
    first = raw_own[...].astype(F32) + summed
    summed = cross[0:half].astype(F32) + cross_head[0:half].astype(F32)
    second = cross[half:].astype(F32) + summed
    low, high = jnp.where(p == 0, first, second), jnp.where(p == 0, second, first)
    places = half // count
    pieces = [v[i : i + places] for i in range(0, half, places) for v in (low, high)]
    after_ref[...] = jnp.concatenate(pieces, axis=0).astype(BF16)
    x = after_ref[...].astype(F32)
    mean = jnp.mean(x, axis=-1, keepdims=True)
    centred = x - mean
    square = jnp.sum(centred * centred, axis=-1, keepdims=True)
    y = (centred * gain_ref[0:1]).astype(BF16)
    width = weight_ref.shape[2]
    last = width // 128 * 128
    for t in range(KINDS):
        total[t, :, 0:width] = jnp.dot(y, weight_ref[t], preferred_element_type=F32)
        tail = total[t, :, last:]
        lane = lax.broadcasted_iota(jnp.int32, tail.shape, 1) - (width - last)
        tail = jnp.where(lane < 0, tail, 0.0)
        if t == 0:
            for at, item in enumerate((*in_three(mean), *in_three(square))):
                tail = jnp.where(lane == at, item, tail)
        total[t, :, last:] = tail
    rows = total.shape[1] // count
    for k in range(count):
        place = pl.multiple_of((f ^ k) * rows, rows)
        for t in range(KINDS):
            outs[k][t] = total.at[t][pl.ds(place, rows), :].astype(BF16)


def attend_space_body(count, share, *refs):
    parts, fixed, out_ref = refs[:count], refs[count : 2 * count], refs[2 * count]
    rows, width = out_ref.shape
    last = width // 128 * 128
    means, squares = [], []
    for k in range(count):
        tail = parts[k][0].astype(F32)[:, last:]
        lane = lax.broadcasted_iota(jnp.int32, tail.shape, 1) - (width - last)
        means.append(
            jnp.sum(jnp.where((lane >= 0) & (lane < 3), tail, 0.0), axis=-1, keepdims=True)
        )
        squares.append(
            jnp.sum(jnp.where((lane >= 3) & (lane < 6), tail, 0.0), axis=-1, keepdims=True)
        )
    mean = sum(means) / count
    square = sum(squares) + share * sum((m - mean) * (m - mean) for m in means)
    scale = lax.rsqrt(square / (share * count) + 1e-06)
    qkv = []
    for t in range(KINDS):
        total = jnp.zeros((rows, width), F32)
        for k in range(count):
            row = fixed[k][...].astype(F32)[rows + t : rows + t + 1]
            total = total + parts[k][t].astype(F32)[:, 0:width] + (means[k] - mean) * row
        qkv.append((total * scale).astype(BF16).astype(F32))
    out_ref[...] = attend_rows(*qkv).astype(BF16)


def out_space_body(count, *refs):
    parts, weight_ref, after_ref = refs[:count], refs[count], refs[count + 1]
    outs, (tokens, total, after) = refs[count + 2 : 2 * count + 2], refs[2 * count + 2 :]
    f = lax.axis_index("frame")
    rows = tokens.shape[0] // count
    for k in range(count):
        place = pl.multiple_of((f ^ k) * rows, rows)
        tokens[pl.ds(place, rows), :] = parts[k][...].astype(F32)
    total[...] = lax.dot_general(
        tokens[...].astype(BF16), weight_ref[...], NT, preferred_element_type=F32
    )
    after[...] = after_ref[...].astype(F32)
    for k in range(count):
        place = pl.multiple_of((f ^ k) * rows, rows)
        value = jnp.concatenate(
            [total[pl.ds(place, rows), :], after[pl.ds(place, rows), :]], axis=0
        )
        outs[k][...] = value.astype(BF16)


def join_body(count, *refs):
    parts, partial_ref, after_ref, held = refs[:count], *refs[count:]
    f = lax.axis_index("frame")
    rows = partial_ref.shape[0]
    for k in range(count):
        held[f ^ k] = parts[k][...].astype(F32)
    whole = jnp.concatenate([held[s] for s in range(count)], axis=1)
    partial_ref[...] = whole[0:rows].astype(BF16)
    after_ref[...] = whole[rows:].astype(BF16)


def finish_body(own, other, after, out_ref):
    out_ref[0] = after[...].astype(F32) + (own[...].astype(F32) + other[...].astype(F32))


def moving_tokens(video, gain_time, qkv_time, out_time, gain_space, qkv_space, out_space):
    count = lax.axis_size("frame")
    frames_here, patches_here, width = video.shape
    share, columns = out_time.shape
    rows = frames_here * patches_here
    plane = rows * count
    padded = (columns // 128 + 1) * 128
    qkv_time, qkv_space = (jnp.transpose(w, (1, 0, 2)) for w in (qkv_time, qkv_space))
    gain_time, gain_space = gain_time.reshape(1, width), gain_space.reshape(1, width)
    body = functools.partial
    swap = [(0, 1), (1, 0)]

    normed = exchange(
        run(
            body(split_body, count),
            [((2 * rows, share), BF16)] * count,
            video,
            gain_time,
            scratch=[((count, 2 * rows, share), F32)],
        )
    )
    partial_time = exchange(
        run(
            body(project_body, count),
            [((KINDS, rows, columns), BF16)] * count,
            *normed,
            qkv_time,
            scratch=[((plane, share), F32), ((KINDS, plane, columns), F32)],
        )
    )
    fixed, gain_own, raw_own, raw_other = run(
        body(prepare_body, count),
        [
            ((8, columns), F32),
            ((8, share), F32),
            ((plane // 2, share), BF16),
            ((plane // 2, share), BF16),
        ],
        *normed,
        gain_space,
        qkv_space,
        scratch=[((count, 8, share), F32), ((count, rows, share), F32)],
    )
    attended = run(
        body(attend_time_body, count), ((rows + 8, columns), BF16), *partial_time, fixed
    )
    attended = exchange([attended] * count)
    own, cross = run(
        body(out_time_body, count),
        [((plane // 2, share), BF16), ((plane, share), BF16)],
        *attended,
        out_time,
        raw_other,
        scratch=[((plane, columns), F32)],
    )
    own_head = lax.ppermute(own, "head", swap)
    crossed = lax.ppermute(cross, "patch", swap)
    cross_head = lax.ppermute(
        cross[: plane // 2], ("patch", "head"), [(i, 3 - i) for i in range(4)]
    )
    *partial_space, after = run(
        body(project_space_body, count),
        [((KINDS, rows, padded), BF16)] * count + [((plane, share), BF16)],
        own,
        own_head,
        crossed,
        cross_head,
        raw_own,
        gain_own,
        qkv_space,
        scratch=[((KINDS, plane, padded), F32)],
    )
    partial_space = exchange(partial_space)
    frame = run(
        body(attend_space_body, count, share),
        ((rows, columns), BF16),
        *partial_space,
        *attended,
    )
    frame = exchange([frame] * count)
    pieces = exchange(
        run(
            body(out_space_body, count),
            [((2 * rows, share), BF16)] * count,
            *frame,
            out_space,
            after,
            scratch=[((plane, columns), F32), ((plane, share), F32), ((plane, share), F32)],
        )
    )
    mine, after = run(
        body(join_body, count),
        [((rows, width), BF16)] * 2,
        *pieces,
        scratch=[((count, 2 * rows, share), F32)],
    )
    theirs = lax.ppermute(mine, "head", swap)
    return run(finish_body, ((1, rows, width), F32), mine, theirs, after)


def solution(mesh):
    placed = (
        P(("groups", "frame"), "patch", None),
        P(),
        P("frame", None, "head"),
        P("frame", "head"),
        P(),
        P("frame", None, "head"),
        P("frame", "head"),
    )

    def program(video, *rest):
        frames_here, patches_here, width = video.shape
        count = lax.axis_size("frame")
        small = (
            patches_here == count
            and frames_here == lax.axis_size("patch") == lax.axis_size("head") == 2
            and frames_here * patches_here == 8
            and frames_here * count * patches_here < width
        )
        return (moving_tokens if small else on_device)(video, *rest)

    return jax.shard_map(
        program,
        mesh=mesh,
        in_specs=placed,
        out_specs=P(("groups", "frame", "patch"), None, None),
        check_vma=False,
    )
```

```python
import functools

import jax
import jax.numpy as jnp
from jax import lax
from jax.experimental import pallas as pl
from jax.experimental.pallas import tpu as pltpu
from jax.sharding import PartitionSpec as P

HEAD_WIDTH = 72


def layer_norm(tokens, gain):
    value_rows = tokens.astype(jnp.float32)
    center = jnp.mean(value_rows, axis=-1, keepdims=True)
    spread = jnp.mean((value_rows - center) ** 2, axis=-1, keepdims=True)
    return ((value_rows - center) * lax.rsqrt(spread + 1e-06) * gain).astype(jnp.bfloat16)


def project_qkv(normed, weight):
    columns = weight.shape[1] * weight.shape[2]
    total = jnp.dot(
        normed, weight.reshape(weight.shape[0], columns), preferred_element_type=jnp.float32
    )
    return total.astype(jnp.bfloat16)


def project_out(attended, weight):
    return lax.dot_general(
        attended, weight, (((1,), (1,)), ((), ())), preferred_element_type=jnp.float32
    )


def attend(qkv, over_first):
    query_rows, key_rows, value_rows = (qkv[:, :, 0], qkv[:, :, 1], qkv[:, :, 2])
    factor = 1.0 / jnp.sqrt(jnp.float32(HEAD_WIDTH))
    if over_first:
        score_matrix = (
            jnp.einsum("abhd,cbhd->bhac", query_rows, key_rows, preferred_element_type=jnp.float32)
            * factor
        )
        attention_weights = jax.nn.softmax(score_matrix, axis=-1).astype(jnp.bfloat16)
        attention_output = jnp.einsum(
            "bhac,cbhd->abhd", attention_weights, value_rows, preferred_element_type=jnp.float32
        )
    else:
        score_matrix = (
            jnp.einsum("abhd,achd->ahbc", query_rows, key_rows, preferred_element_type=jnp.float32)
            * factor
        )
        attention_weights = jax.nn.softmax(score_matrix, axis=-1).astype(jnp.bfloat16)
        attention_output = jnp.einsum(
            "ahbc,achd->abhd", attention_weights, value_rows, preferred_element_type=jnp.float32
        )
    return attention_output.astype(jnp.bfloat16)


def mix_partial(tokens, gain, qkv_weight, out_weight, over_first):
    rows_a, rows_b, width = tokens.shape
    flat = tokens.reshape(rows_a * rows_b, width)
    normed = layer_norm(flat, gain)
    qkv = project_qkv(normed, qkv_weight).reshape(rows_a, rows_b, 3, -1, HEAD_WIDTH)
    attended = attend(qkv, over_first).reshape(rows_a * rows_b, -1)
    partial_value = project_out(attended, out_weight)
    rounded = lax.optimization_barrier(partial_value.astype(jnp.bfloat16)).astype(jnp.float32)
    return (flat, rounded)


def on_device(video, gain_time, qkv_time, out_time, gain_space, qkv_space, out_space):
    frame_size = lax.axis_size("frame")
    patch_size = lax.axis_size("patch")
    device_count = frame_size * patch_size
    series = lax.all_to_all(video, "frame", split_axis=1, concat_axis=0, tiled=True)
    qkv_time, out_time, qkv_space, out_space = (
        lax.all_gather(qkv_time, "frame", axis=0, tiled=True),
        lax.all_gather(out_time, "frame", axis=0, tiled=True),
        lax.all_gather(qkv_space, "frame", axis=0, tiled=True),
        lax.all_gather(out_space, "frame", axis=0, tiled=True),
    )
    frame_count, series_count, width = series.shape
    set_count = frame_count // device_count
    flat, rounded = mix_partial(series, gain_time, qkv_time, out_time, True)
    summed = (
        lax.psum(rounded.astype(jnp.bfloat16), "head")
        .astype(jnp.float32)
        .reshape(device_count, set_count, series_count, width)
    )
    resident = flat.reshape(device_count, set_count, series_count, width)
    after_time = (resident.astype(jnp.float32) + summed).astype(jnp.bfloat16)
    arrived = lax.all_to_all(
        after_time, ("frame", "patch"), split_axis=0, concat_axis=2, tiled=True
    )
    whole_frames = arrived.reshape(set_count, device_count * series_count, width)
    whole_frames = whole_frames.reshape(set_count, frame_size, patch_size, series_count, width)
    whole_frames = jnp.transpose(whole_frames, (0, 2, 1, 3, 4)).reshape(
        set_count, device_count * series_count, width
    )
    flat_space, rounded_space = mix_partial(whole_frames, gain_space, qkv_space, out_space, False)
    summed_space = lax.psum(rounded_space.astype(jnp.bfloat16), "head").astype(jnp.float32)
    result = flat_space.astype(jnp.float32) + summed_space
    return result.reshape(whole_frames.shape)


F32 = jnp.float32
BF16 = jnp.bfloat16
KINDS = 3
NT = (((1,), (1,)), ((), ()))


def run(body, outs, *args, scratch=()):
    vmem = pl.BlockSpec(memory_space=pltpu.VMEM)
    single = not isinstance(outs, list)
    shapes = [jax.ShapeDtypeStruct(*o) for o in ([outs] if single else outs)]
    found = pl.pallas_call(
        body,
        out_shape=shapes,
        in_specs=[vmem] * len(args),
        out_specs=[vmem] * len(shapes),
        scratch_shapes=[pltpu.VMEM(*s) for s in scratch],
        compiler_params=pltpu.CompilerParams(vmem_limit_bytes=16 << 20),
    )(*args)
    return found[0] if single else found


def lanes(value, start, size):
    return lax.slice_in_dim(value, start, start + size, axis=1)


def exchange(messages):
    count = len(messages)
    return [messages[0]] + [
        lax.ppermute(messages[k], "frame", [(i, i ^ k) for i in range(count)])
        for k in range(1, count)
    ]


def pick_rows(value, source):
    column = lax.broadcasted_iota(jnp.int32, (source.shape[0], value.shape[0]), 1)
    chosen = jnp.where(column == source, 1.0, 0.0).astype(BF16)
    return jnp.dot(chosen, value.astype(BF16), preferred_element_type=F32)


def split_body(count, video_ref, gain_ref, *refs):
    outs, held = refs[:count], refs[count]
    f = lax.axis_index("frame")
    rows = video_ref.shape[0] * video_ref.shape[1]
    share = held.shape[2]
    x = jnp.concatenate([video_ref[i].astype(F32) for i in range(video_ref.shape[0])], axis=0)
    mean = jnp.mean(x, axis=-1, keepdims=True)
    centred = x - mean
    spread = jnp.mean(centred * centred, axis=-1, keepdims=True)
    y = centred * lax.rsqrt(spread + 1e-06) * gain_ref[...]
    for s in range(count):
        held[s, 0:rows] = lanes(y, s * share, share)
        held[s, rows:] = lanes(x, s * share, share)
    for k in range(count):
        outs[k][...] = held[f ^ k].astype(BF16)


def project_body(count, *refs):
    parts, weight_ref, outs = refs[:count], refs[count], refs[count + 1 : 2 * count + 1]
    tokens, total = refs[2 * count + 1 :]
    f = lax.axis_index("frame")
    rows = tokens.shape[0] // count
    for k in range(count):
        place = pl.multiple_of((f ^ k) * rows, rows)
        tokens[pl.ds(place, rows), :] = parts[k][0:rows].astype(F32)
    row = lax.broadcasted_iota(jnp.int32, (tokens.shape[0], 1), 0)
    source = lax.rem(row, rows) * count + lax.div(row, rows)
    x = pick_rows(tokens[...], source).astype(BF16)
    for t in range(KINDS):
        total[t] = jnp.dot(x, weight_ref[t], preferred_element_type=F32)
    for k in range(count):
        place = pl.multiple_of((f ^ k) * rows, rows)
        for t in range(KINDS):
            outs[k][t] = total.at[t][pl.ds(place, rows), :].astype(BF16)


def prepare_body(count, *refs):
    parts, gain_ref, weight_ref = refs[:count], refs[count], refs[count + 1]
    fixed_ref, gain_own, raw_own, raw_other, gains, raw = refs[count + 2 :]
    f, p = lax.axis_index("frame"), lax.axis_index("patch")
    share = gains.shape[2]
    for s in range(count):
        gains[s] = jnp.broadcast_to(lanes(gain_ref[...], s * share, share), gains.shape[1:])
    g = gains[f]
    gain_own[...] = g
    g = g.astype(BF16)
    rows = [jnp.dot(g, weight_ref[t], preferred_element_type=F32) for t in range(KINDS)]
    row = lax.broadcasted_iota(jnp.int32, rows[0].shape, 0)
    fixed_ref[...] = jnp.where(row == 0, rows[0], jnp.where(row == 1, rows[1], rows[2]))
    whole = parts[0].shape[0] // 2
    places = whole // 2
    for k in range(count):
        raw[f ^ k] = parts[k][whole:].astype(F32)
    even, odd = (
        jnp.concatenate([raw[s][at : at + places] for s in range(count)], axis=0)
        for at in (0, places)
    )
    raw_own[...] = jnp.where(p == 0, even, odd).astype(BF16)
    raw_other[...] = jnp.where(p == 0, odd, even).astype(BF16)


def attend_rows(query, key, value):
    rows, width = query.shape
    heads = width // HEAD_WIDTH
    spread = heads * rows
    first = lax.broadcasted_iota(jnp.int32, (heads, rows, width), 0) * HEAD_WIDTH
    first = first.reshape(spread, width)
    lane = lax.broadcasted_iota(jnp.int32, (spread, width), 1)
    mine = (lane >= first) & (lane < first + HEAD_WIDTH)
    keys = jnp.where(mine, jnp.concatenate([key] * heads, axis=0), 0.0).astype(BF16)
    values = jnp.where(mine, jnp.concatenate([value] * heads, axis=0), 0.0).astype(BF16)
    scores = lax.dot_general(keys, query.astype(BF16), NT, preferred_element_type=F32)
    scores = (scores * (1.0 / HEAD_WIDTH**0.5)).reshape(heads, rows, rows)
    power = jnp.exp(scores - jnp.max(scores, axis=1, keepdims=True))
    weights = power / jnp.sum(power, axis=1, keepdims=True)
    weights = weights.reshape(spread, rows).T.astype(BF16)
    return jnp.dot(weights, values, preferred_element_type=F32)


def attend_time_body(count, *refs):
    parts, fixed_ref, out_ref = refs[:count], refs[count], refs[count + 1]
    qkv = []
    for t in range(KINDS):
        total = parts[0][t].astype(F32)
        for k in range(1, count):
            total = total + parts[k][t].astype(F32)
        qkv.append(total.astype(BF16).astype(F32))
    attended = attend_rows(*qkv)
    out_ref[...] = jnp.concatenate([attended, fixed_ref[...]], axis=0).astype(BF16)


def out_time_body(count, *refs):
    parts, weight_ref, raw_other = refs[:count], refs[count], refs[count + 1]
    own_ref, other_ref, tokens = refs[count + 2 :]
    f, p = lax.axis_index("frame"), lax.axis_index("patch")
    rows = tokens.shape[0] // count
    for k in range(count):
        place = pl.multiple_of((f ^ k) * rows, rows)
        tokens[pl.ds(place, rows), :] = parts[k][0:rows].astype(F32)
    half = tokens.shape[0] // 2
    row = lax.broadcasted_iota(jnp.int32, (tokens.shape[0], 1), 0)
    parity = jnp.where(row < half, p, 1 - p)
    row = lax.rem(row, half)
    source = lax.rem(row, count) * rows + 2 * lax.div(row, count) + parity
    x = pick_rows(tokens[...], source).astype(BF16)
    total = lax.dot_general(x, weight_ref[...], NT, preferred_element_type=F32)
    own_ref[...] = total[0:half].astype(BF16)
    other_ref[0:half] = total[half:].astype(BF16)
    other_ref[half:] = raw_other[...]


def in_three(value):
    high = value.astype(BF16).astype(F32)
    middle = (value - high).astype(BF16).astype(F32)
    return high, middle, value - high - middle


def project_space_body(count, *refs):
    own, own_head, cross, cross_head, raw_own, gain_ref, weight_ref = refs[:7]
    outs, after_ref, total = refs[7 : 7 + count], *refs[7 + count :]
    f, p = lax.axis_index("frame"), lax.axis_index("patch")
    half = own.shape[0]
    summed = own[...].astype(F32) + own_head[...].astype(F32)
    first = raw_own[...].astype(F32) + summed
    summed = cross[0:half].astype(F32) + cross_head[0:half].astype(F32)
    second = cross[half:].astype(F32) + summed
    low, high = jnp.where(p == 0, first, second), jnp.where(p == 0, second, first)
    places = half // count
    pieces = [v[i : i + places] for i in range(0, half, places) for v in (low, high)]
    after_ref[...] = jnp.concatenate(pieces, axis=0).astype(BF16)
    x = after_ref[...].astype(F32)
    mean = jnp.mean(x, axis=-1, keepdims=True)
    centred = x - mean
    square = jnp.sum(centred * centred, axis=-1, keepdims=True)
    y = (centred * gain_ref[0:1]).astype(BF16)
    width = weight_ref.shape[2]
    last = width // 128 * 128
    for t in range(KINDS):
        total[t, :, 0:width] = jnp.dot(y, weight_ref[t], preferred_element_type=F32)
        tail = total[t, :, last:]
        lane = lax.broadcasted_iota(jnp.int32, tail.shape, 1) - (width - last)
        tail = jnp.where(lane < 0, tail, 0.0)
        if t == 0:
            for at, item in enumerate((*in_three(mean), *in_three(square))):
                tail = jnp.where(lane == at, item, tail)
        total[t, :, last:] = tail
    rows = total.shape[1] // count
    for k in range(count):
        place = pl.multiple_of((f ^ k) * rows, rows)
        for t in range(KINDS):
            outs[k][t] = total.at[t][pl.ds(place, rows), :].astype(BF16)


def attend_space_body(count, share, *refs):
    parts, fixed, out_ref = refs[:count], refs[count : 2 * count], refs[2 * count]
    rows, width = out_ref.shape
    last = width // 128 * 128
    means, squares = [], []
    for k in range(count):
        tail = parts[k][0].astype(F32)[:, last:]
        lane = lax.broadcasted_iota(jnp.int32, tail.shape, 1) - (width - last)
        means.append(
            jnp.sum(jnp.where((lane >= 0) & (lane < 3), tail, 0.0), axis=-1, keepdims=True)
        )
        squares.append(
            jnp.sum(jnp.where((lane >= 3) & (lane < 6), tail, 0.0), axis=-1, keepdims=True)
        )
    mean = sum(means) / count
    square = sum(squares) + share * sum((m - mean) * (m - mean) for m in means)
    scale = lax.rsqrt(square / (share * count) + 1e-06)
    qkv = []
    for t in range(KINDS):
        total = jnp.zeros((rows, width), F32)
        for k in range(count):
            row = fixed[k][...].astype(F32)[rows + t : rows + t + 1]
            total = total + parts[k][t].astype(F32)[:, 0:width] + (means[k] - mean) * row
        qkv.append((total * scale).astype(BF16).astype(F32))
    out_ref[...] = attend_rows(*qkv).astype(BF16)


def out_space_body(count, *refs):
    parts, weight_ref, after_ref = refs[:count], refs[count], refs[count + 1]
    outs, (tokens, total, after) = refs[count + 2 : 2 * count + 2], refs[2 * count + 2 :]
    f = lax.axis_index("frame")
    rows = tokens.shape[0] // count
    for k in range(count):
        place = pl.multiple_of((f ^ k) * rows, rows)
        tokens[pl.ds(place, rows), :] = parts[k][...].astype(F32)
    total[...] = lax.dot_general(
        tokens[...].astype(BF16), weight_ref[...], NT, preferred_element_type=F32
    )
    after[...] = after_ref[...].astype(F32)
    for k in range(count):
        place = pl.multiple_of((f ^ k) * rows, rows)
        value = jnp.concatenate(
            [total[pl.ds(place, rows), :], after[pl.ds(place, rows), :]], axis=0
        )
        outs[k][...] = value.astype(BF16)


def join_body(count, *refs):
    parts, partial_ref, after_ref, held = refs[:count], *refs[count:]
    f = lax.axis_index("frame")
    rows = partial_ref.shape[0]
    for k in range(count):
        held[f ^ k] = parts[k][...].astype(F32)
    whole = jnp.concatenate([held[s] for s in range(count)], axis=1)
    partial_ref[...] = whole[0:rows].astype(BF16)
    after_ref[...] = whole[rows:].astype(BF16)


def finish_body(own, other, after, out_ref):
    out_ref[0] = after[...].astype(F32) + (own[...].astype(F32) + other[...].astype(F32))


def moving_tokens(video, gain_time, qkv_time, out_time, gain_space, qkv_space, out_space):
    count = lax.axis_size("frame")
    frames_here, patches_here, width = video.shape
    share, columns = out_time.shape
    rows = frames_here * patches_here
    plane = rows * count
    padded = (columns // 128 + 1) * 128
    qkv_time, qkv_space = (jnp.transpose(w, (1, 0, 2)) for w in (qkv_time, qkv_space))
    gain_time, gain_space = gain_time.reshape(1, width), gain_space.reshape(1, width)
    body = functools.partial
    swap = [(0, 1), (1, 0)]

    normed = exchange(
        run(
            body(split_body, count),
            [((2 * rows, share), BF16)] * count,
            video,
            gain_time,
            scratch=[((count, 2 * rows, share), F32)],
        )
    )
    partial_time = exchange(
        run(
            body(project_body, count),
            [((KINDS, rows, columns), BF16)] * count,
            *normed,
            qkv_time,
            scratch=[((plane, share), F32), ((KINDS, plane, columns), F32)],
        )
    )
    fixed, gain_own, raw_own, raw_other = run(
        body(prepare_body, count),
        [
            ((8, columns), F32),
            ((8, share), F32),
            ((plane // 2, share), BF16),
            ((plane // 2, share), BF16),
        ],
        *normed,
        gain_space,
        qkv_space,
        scratch=[((count, 8, share), F32), ((count, rows, share), F32)],
    )
    attended = run(
        body(attend_time_body, count), ((rows + 8, columns), BF16), *partial_time, fixed
    )
    attended = exchange([attended] * count)
    own, cross = run(
        body(out_time_body, count),
        [((plane // 2, share), BF16), ((plane, share), BF16)],
        *attended,
        out_time,
        raw_other,
        scratch=[((plane, columns), F32)],
    )
    own_head = lax.ppermute(own, "head", swap)
    crossed = lax.ppermute(cross, "patch", swap)
    cross_head = lax.ppermute(
        cross[: plane // 2], ("patch", "head"), [(i, 3 - i) for i in range(4)]
    )
    *partial_space, after = run(
        body(project_space_body, count),
        [((KINDS, rows, padded), BF16)] * count + [((plane, share), BF16)],
        own,
        own_head,
        crossed,
        cross_head,
        raw_own,
        gain_own,
        qkv_space,
        scratch=[((KINDS, plane, padded), F32)],
    )
    partial_space = exchange(partial_space)
    frame = run(
        body(attend_space_body, count, share),
        ((rows, columns), BF16),
        *partial_space,
        *attended,
    )
    frame = exchange([frame] * count)
    pieces = exchange(
        run(
            body(out_space_body, count),
            [((2 * rows, share), BF16)] * count,
            *frame,
            out_space,
            after,
            scratch=[((plane, columns), F32), ((plane, share), F32), ((plane, share), F32)],
        )
    )
    mine, after = run(
        body(join_body, count),
        [((rows, width), BF16)] * 2,
        *pieces,
        scratch=[((count, 2 * rows, share), F32)],
    )
    theirs = lax.ppermute(mine, "head", swap)
    return run(finish_body, ((1, rows, width), F32), mine, theirs, after)


def solution(mesh):
    placed = (
        P(("groups", "frame"), "patch", None),
        P(),
        P("frame", None, "head"),
        P("frame", "head"),
        P(),
        P("frame", None, "head"),
        P("frame", "head"),
    )

    def program(video, *rest):
        frames_here, patches_here, width = video.shape
        count = lax.axis_size("frame")
        small = (
            patches_here == count
            and frames_here == lax.axis_size("patch") == lax.axis_size("head") == 2
            and frames_here * patches_here == 8
            and frames_here * count * patches_here < width
        )
        return (moving_tokens if small else on_device)(video, *rest)

    return jax.shard_map(
        program,
        mesh=mesh,
        in_specs=placed,
        out_specs=P(("groups", "frame", "patch"), None, None),
        check_vma=False,
    )
```

```python
import functools

import jax
import jax.numpy as jnp
from jax import lax
from jax.experimental import pallas as pl
from jax.experimental.pallas import tpu as pltpu


from jax.sharding import PartitionSpec as P

HEAD_WIDTH = 72


def layer_norm(tokens, gain):
    value_rows = tokens.astype(jnp.float32)
    center = jnp.mean(value_rows, axis=-1, keepdims=True)
    spread = jnp.mean((value_rows - center) ** 2, axis=-1, keepdims=True)
    return ((value_rows - center) * lax.rsqrt(spread + 1e-06) * gain).astype(jnp.bfloat16)


def project_qkv(normed, weight):
    columns = weight.shape[1] * weight.shape[2]
    total = jnp.dot(
        normed, weight.reshape(weight.shape[0], columns), preferred_element_type=jnp.float32
    )
    return total.astype(jnp.bfloat16)


def project_out(attended, weight):
    return lax.dot_general(
        attended, weight, (((1,), (1,)), ((), ())), preferred_element_type=jnp.float32
    )


def attend(qkv, over_first):
    query_rows, key_rows, value_rows = (qkv[:, :, 0], qkv[:, :, 1], qkv[:, :, 2])
    factor = 1.0 / jnp.sqrt(jnp.float32(HEAD_WIDTH))
    if over_first:
        score_matrix = (
            jnp.einsum("abhd,cbhd->bhac", query_rows, key_rows, preferred_element_type=jnp.float32)
            * factor
        )
        attention_weights = jax.nn.softmax(score_matrix, axis=-1).astype(jnp.bfloat16)
        attention_output = jnp.einsum(
            "bhac,cbhd->abhd", attention_weights, value_rows, preferred_element_type=jnp.float32
        )
    else:
        score_matrix = (
            jnp.einsum("abhd,achd->ahbc", query_rows, key_rows, preferred_element_type=jnp.float32)
            * factor
        )
        attention_weights = jax.nn.softmax(score_matrix, axis=-1).astype(jnp.bfloat16)
        attention_output = jnp.einsum(
            "ahbc,achd->abhd", attention_weights, value_rows, preferred_element_type=jnp.float32
        )
    return attention_output.astype(jnp.bfloat16)


def mix_partial(tokens, gain, qkv_weight, out_weight, over_first):
    rows_a, rows_b, width = tokens.shape
    flat = tokens.reshape(rows_a * rows_b, width)
    normed = layer_norm(flat, gain)
    qkv = project_qkv(normed, qkv_weight).reshape(rows_a, rows_b, 3, -1, HEAD_WIDTH)
    attended = attend(qkv, over_first).reshape(rows_a * rows_b, -1)
    partial_value = project_out(attended, out_weight)
    rounded = lax.optimization_barrier(partial_value.astype(jnp.bfloat16)).astype(jnp.float32)
    return (flat, rounded)


def on_device(video, gain_time, qkv_time, out_time, gain_space, qkv_space, out_space):
    frame_size = lax.axis_size("frame")
    patch_size = lax.axis_size("patch")
    device_count = frame_size * patch_size
    series = lax.all_to_all(video, "frame", split_axis=1, concat_axis=0, tiled=True)
    qkv_time, out_time, qkv_space, out_space = (
        lax.all_gather(qkv_time, "frame", axis=0, tiled=True),
        lax.all_gather(out_time, "frame", axis=0, tiled=True),
        lax.all_gather(qkv_space, "frame", axis=0, tiled=True),
        lax.all_gather(out_space, "frame", axis=0, tiled=True),
    )
    frame_count, series_count, width = series.shape
    set_count = frame_count // device_count
    flat, rounded = mix_partial(series, gain_time, qkv_time, out_time, True)
    summed = (
        lax.psum(rounded.astype(jnp.bfloat16), "head")
        .astype(jnp.float32)
        .reshape(device_count, set_count, series_count, width)
    )
    resident = flat.reshape(device_count, set_count, series_count, width)
    after_time = (resident.astype(jnp.float32) + summed).astype(jnp.bfloat16)
    arrived = lax.all_to_all(
        after_time, ("frame", "patch"), split_axis=0, concat_axis=2, tiled=True
    )
    whole_frames = arrived.reshape(set_count, device_count * series_count, width)
    whole_frames = whole_frames.reshape(set_count, frame_size, patch_size, series_count, width)
    whole_frames = jnp.transpose(whole_frames, (0, 2, 1, 3, 4)).reshape(
        set_count, device_count * series_count, width
    )
    flat_space, rounded_space = mix_partial(whole_frames, gain_space, qkv_space, out_space, False)
    summed_space = lax.psum(rounded_space.astype(jnp.bfloat16), "head").astype(jnp.float32)
    result = flat_space.astype(jnp.float32) + summed_space
    return result.reshape(whole_frames.shape)


F32 = jnp.float32
BF16 = jnp.bfloat16
KINDS = 3
NT = (((1,), (1,)), ((), ()))


def run(body, outs, *args, scratch=()):
    vmem = pl.BlockSpec(memory_space=pltpu.VMEM)
    single = not isinstance(outs, list)
    shapes = [jax.ShapeDtypeStruct(*o) for o in ([outs] if single else outs)]
    found = pl.pallas_call(
        body,
        out_shape=shapes,
        in_specs=[vmem] * len(args),
        out_specs=[vmem] * len(shapes),
        scratch_shapes=[pltpu.VMEM(*s) for s in scratch],
        compiler_params=pltpu.CompilerParams(vmem_limit_bytes=16 << 20),
    )(*args)
    return found[0] if single else found


def lanes(value, start, size):
    return lax.slice_in_dim(value, start, start + size, axis=1)


def exchange(messages):
    count = len(messages)
    return [messages[0]] + [
        lax.ppermute(messages[k], "frame", [(i, i ^ k) for i in range(count)])
        for k in range(1, count)
    ]


def pick_rows(value, source):
    column = lax.broadcasted_iota(jnp.int32, (source.shape[0], value.shape[0]), 1)
    chosen = jnp.where(column == source, 1.0, 0.0).astype(BF16)
    return jnp.dot(chosen, value.astype(BF16), preferred_element_type=F32)


def split_body(count, video_ref, gain_ref, *refs):
    outs, held = refs[:count], refs[count]
    f = lax.axis_index("frame")
    rows = video_ref.shape[0] * video_ref.shape[1]
    share = held.shape[2]
    x = jnp.concatenate([video_ref[i].astype(F32) for i in range(video_ref.shape[0])], axis=0)
    mean = jnp.mean(x, axis=-1, keepdims=True)
    centred = x - mean
    spread = jnp.mean(centred * centred, axis=-1, keepdims=True)
    y = centred * lax.rsqrt(spread + 1e-06) * gain_ref[...].reshape(1, -1)
    for s in range(count):
        held[s, 0:rows] = lanes(y, s * share, share)
        held[s, rows:] = lanes(x, s * share, share)
    for k in range(count):
        outs[k][...] = held[f ^ k].astype(BF16)


def project_body(count, *refs):
    parts, weight_ref, outs = refs[:count], refs[count], refs[count + 1 : 2 * count + 1]
    tokens, total = refs[2 * count + 1 :]
    f = lax.axis_index("frame")
    rows = tokens.shape[0] // count
    for k in range(count):
        place = pl.multiple_of((f ^ k) * rows, rows)
        tokens[pl.ds(place, rows), :] = parts[k][0:rows].astype(F32)
    row = lax.broadcasted_iota(jnp.int32, (tokens.shape[0], 1), 0)
    source = lax.rem(row, rows) * count + lax.div(row, rows)
    x = pick_rows(tokens[...], source).astype(BF16)
    for t in range(KINDS):
        total[t] = jnp.dot(x, weight_ref[t], preferred_element_type=F32)
    for k in range(count):
        place = pl.multiple_of((f ^ k) * rows, rows)
        for t in range(KINDS):
            outs[k][t] = total.at[t][pl.ds(place, rows), :].astype(BF16)


def prepare_body(count, *refs):
    parts, gain_ref, weight_ref = refs[:count], refs[count], refs[count + 1]
    fixed_ref, gain_own, raw_own, raw_other, gains, raw = refs[count + 2 :]
    f, p = lax.axis_index("frame"), lax.axis_index("patch")
    share = gains.shape[2]
    for s in range(count):
        gains[s] = jnp.broadcast_to(lanes(gain_ref[...].reshape(1, -1), s * share, share), gains.shape[1:])
    g = gains[f]
    gain_own[...] = g
    g = g.astype(BF16)
    rows = [jnp.dot(g, weight_ref[t], preferred_element_type=F32) for t in range(KINDS)]
    row = lax.broadcasted_iota(jnp.int32, rows[0].shape, 0)
    fixed_ref[...] = jnp.where(row == 0, rows[0], jnp.where(row == 1, rows[1], rows[2]))
    whole = parts[0].shape[0] // 2
    places = whole // 2
    for k in range(count):
        raw[f ^ k] = parts[k][whole:].astype(F32)
    even, odd = (
        jnp.concatenate([raw[s][at : at + places] for s in range(count)], axis=0)
        for at in (0, places)
    )
    raw_own[...] = jnp.where(p == 0, even, odd).astype(BF16)
    raw_other[...] = jnp.where(p == 0, odd, even).astype(BF16)


def attend_rows(query, key, value):
    rows, width = query.shape
    heads = width // HEAD_WIDTH
    spread = heads * rows
    first = lax.broadcasted_iota(jnp.int32, (heads, rows, width), 0) * HEAD_WIDTH
    first = first.reshape(spread, width)
    lane = lax.broadcasted_iota(jnp.int32, (spread, width), 1)
    mine = (lane >= first) & (lane < first + HEAD_WIDTH)
    keys = jnp.where(mine, jnp.concatenate([key] * heads, axis=0), 0.0).astype(BF16)
    values = jnp.where(mine, jnp.concatenate([value] * heads, axis=0), 0.0).astype(BF16)
    scores = lax.dot_general(keys, query.astype(BF16), NT, preferred_element_type=F32)
    scores = (scores * (1.0 / HEAD_WIDTH**0.5)).reshape(heads, rows, rows)
    power = jnp.exp(scores - jnp.max(scores, axis=1, keepdims=True))
    weights = power / jnp.sum(power, axis=1, keepdims=True)
    weights = weights.reshape(spread, rows).T.astype(BF16)
    return jnp.dot(weights, values, preferred_element_type=F32)


def attend_time_body(count, *refs):
    parts, fixed_ref, out_ref = refs[:count], refs[count], refs[count + 1]
    qkv = []
    for t in range(KINDS):
        total = parts[0][t].astype(F32)
        for k in range(1, count):
            total = total + parts[k][t].astype(F32)
        qkv.append(total.astype(BF16).astype(F32))
    attended = attend_rows(*qkv)
    out_ref[...] = jnp.concatenate([attended, fixed_ref[...]], axis=0).astype(BF16)


def out_time_body(count, *refs):
    parts, weight_ref, raw_other = refs[:count], refs[count], refs[count + 1]
    own_ref, other_ref, alone_ref, tokens = refs[count + 2 :]
    f, p = lax.axis_index("frame"), lax.axis_index("patch")
    rows = tokens.shape[0] // count
    for k in range(count):
        place = pl.multiple_of((f ^ k) * rows, rows)
        tokens[pl.ds(place, rows), :] = parts[k][0:rows].astype(F32)
    half = tokens.shape[0] // 2
    row = lax.broadcasted_iota(jnp.int32, (tokens.shape[0], 1), 0)
    parity = jnp.where(row < half, p, 1 - p)
    row = lax.rem(row, half)
    source = lax.rem(row, count) * rows + 2 * lax.div(row, count) + parity
    x = pick_rows(tokens[...], source).astype(BF16)
    total = lax.dot_general(x, weight_ref[...], NT, preferred_element_type=F32)
    own_ref[...] = total[0:half].astype(BF16)
    other_ref[0:half] = total[half:].astype(BF16)
    alone_ref[...] = total[half:].astype(BF16)
    other_ref[half:] = raw_other[...]


def in_three(value):
    high = value.astype(BF16).astype(F32)
    middle = (value - high).astype(BF16).astype(F32)
    return high, middle, value - high - middle


def project_space_body(count, *refs):
    own, own_head, cross, cross_head, raw_own, gain_ref, weight_ref = refs[:7]
    outs, total = refs[7 : 7 + count], refs[7 + count]
    f, p = lax.axis_index("frame"), lax.axis_index("patch")
    half = own.shape[0]
    summed = own[...].astype(F32) + own_head[...].astype(F32)
    first = raw_own[...].astype(F32) + summed
    summed = cross[0:half].astype(F32) + cross_head[...].astype(F32)
    second = cross[half:].astype(F32) + summed
    low, high = jnp.where(p == 0, first, second), jnp.where(p == 0, second, first)
    places = half // count
    pieces = [v[i : i + places] for i in range(0, half, places) for v in (low, high)]
    x = jnp.concatenate(pieces, axis=0).astype(BF16).astype(F32)
    mean = jnp.mean(x, axis=-1, keepdims=True)
    centred = x - mean
    square = jnp.sum(centred * centred, axis=-1, keepdims=True)
    y = (centred * gain_ref[0:1]).astype(BF16)
    found = [jnp.dot(y, weight_ref[t], preferred_element_type=F32) for t in range(KINDS)]
    spare = total.shape[1] - KINDS * weight_ref.shape[2] - x.shape[1]
    lane = lax.broadcasted_iota(jnp.int32, (x.shape[0], spare), 1)
    tail = jnp.zeros(lane.shape, F32)
    for at, item in enumerate((*in_three(mean), *in_three(square))):
        tail = jnp.where(lane == at, item, tail)
    total[...] = jnp.concatenate([*found, x, tail], axis=1)
    rows = total.shape[0] // count
    for k in range(count):
        place = pl.multiple_of((f ^ k) * rows, rows)
        outs[k][...] = total[pl.ds(place, rows), :].astype(BF16)


def attend_space_body(count, *refs):
    parts, fixed, refs = refs[:count], refs[count : 2 * count], refs[2 * count :]
    weight_ref, partial_ref, after_ref, held = refs
    f = lax.axis_index("frame")
    rows, columns = parts[0].shape[0], weight_ref.shape[1]
    share = weight_ref.shape[0] // count
    messages = [part[...].astype(F32) for part in parts]
    tails = [lanes(m, KINDS * columns + share, m.shape[1] - KINDS * columns - share) for m in messages]
    lane = lax.broadcasted_iota(jnp.int32, tails[0].shape, 1)
    means = [jnp.sum(jnp.where(lane < 3, t, 0.0), axis=-1, keepdims=True) for t in tails]
    squares = [
        jnp.sum(jnp.where((lane >= 3) & (lane < 6), t, 0.0), axis=-1, keepdims=True) for t in tails
    ]
    mean = sum(means) / count
    square = sum(squares) + share * sum((m - mean) * (m - mean) for m in means)
    scale = lax.rsqrt(square / (share * count) + 1e-06)
    total = sum(messages)
    qkv = []
    for t in range(KINDS):
        value = lanes(total, t * columns, columns)
        for k in range(count):
            value = value + (means[k] - mean) * fixed[k][...].astype(F32)[rows + t : rows + t + 1]
        qkv.append((value * scale).astype(BF16).astype(F32))
    attended = attend_rows(*qkv).astype(BF16)
    for k in range(count):
        held[f ^ k] = lanes(messages[k], KINDS * columns, share)
    partial_ref[...] = lax.dot_general(
        attended, weight_ref[...], NT, preferred_element_type=F32
    ).astype(BF16)
    after_ref[...] = jnp.concatenate([held[s] for s in range(count)], axis=1).astype(BF16)


def assemble_body(count, own, near, side, far, last, out_ref):
    f, p, g = lax.axis_index("frame"), lax.axis_index("patch"), lax.axis_index("groups")
    share, quarter = own.shape[0], own.shape[0] // 4
    out_ref[pl.ds(pl.multiple_of(f * share, share), share), :] = own[...]
    for k in range(1, count):
        for piece, q in (
            (near, 2 * p + g),
            (side, 2 * (1 - p) + g),
            (far, 2 * p + 1 - g),
            (last, 2 * (1 - p) + 1 - g),
        ):
            place = pl.multiple_of((f ^ k) * share + q * quarter, quarter)
            out_ref[pl.ds(place, quarter), :] = piece[(k - 1) * quarter : k * quarter]


def finish_body(own, other, after, out_ref):
    out_ref[0] = after[...].astype(F32) + (own[...].astype(F32) + other[...].astype(F32))


def moving_tokens(video, gain_time, qkv_time, out_time, gain_space, qkv_space, out_space):
    count = lax.axis_size("frame")
    frames_here, patches_here, width = video.shape
    share, columns = out_time.shape
    rows = frames_here * patches_here
    plane = rows * count
    message = (KINDS * columns + share) // 128 * 128 + 128
    qkv_time, qkv_space = (jnp.transpose(w, (1, 0, 2)) for w in (qkv_time, qkv_space))
    body = functools.partial
    swap = [(0, 1), (1, 0)]

    normed = run(
        body(split_body, count),
        [((2 * rows, share), BF16)] * count,
        video,
        gain_time,
        scratch=[((count, 2 * rows, share), F32)],
    )
    normed = exchange(normed)
    partial_time = run(
        body(project_body, count),
        [((KINDS, rows, columns), BF16)] * count,
        *normed,
        qkv_time,
        scratch=[((plane, share), F32), ((KINDS, plane, columns), F32)],
    )
    partial_time = exchange(partial_time)
    quarter = 2 * lax.axis_index("patch") + lax.axis_index("groups")
    piece = lax.dynamic_slice_in_dim(out_space, quarter * (share // 4), share // 4)
    near = jnp.concatenate(exchange([piece] * count)[1:], axis=0)
    side = lax.ppermute(near, "patch", swap)
    far, last = (lax.ppermute(v, "groups", swap) for v in (near, side))
    whole_space = run(
        body(assemble_body, count), ((width, columns), BF16), out_space, near, side, far, last
    )
    fixed, gain_own, raw_own, raw_other = run(
        body(prepare_body, count),
        [
            ((8, columns), F32),
            ((8, share), F32),
            ((plane // 2, share), BF16),
            ((plane // 2, share), BF16),
        ],
        *normed,
        gain_space,
        qkv_space,
        scratch=[((count, 8, share), F32), ((count, rows, share), F32)],
    )
    attended = run(
        body(attend_time_body, count), ((rows + 8, columns), BF16), *partial_time, fixed
    )
    attended = exchange([attended] * count)
    own, cross, cross_only = run(
        body(out_time_body, count),
        [((plane // 2, share), BF16), ((plane, share), BF16), ((plane // 2, share), BF16)],
        *attended,
        out_time,
        raw_other,
        scratch=[((plane, columns), F32)],
    )
    own_head = lax.ppermute(own, "head", swap)
    crossed = lax.ppermute(cross, "patch", swap)
    cross_head = lax.ppermute(cross_only, ("patch", "head"), [(i, 3 - i) for i in range(4)])
    partial_space = run(
        body(project_space_body, count),
        [((rows, message), BF16)] * count,
        own,
        own_head,
        crossed,
        cross_head,
        raw_own,
        gain_own,
        qkv_space,
        scratch=[((plane, message), F32)],
    )
    partial_space = exchange(partial_space)
    mine, after = run(
        body(attend_space_body, count),
        [((rows, width), BF16)] * 2,
        *partial_space,
        *attended,
        whole_space,
        scratch=[((count, rows, share), F32)],
    )
    theirs = lax.ppermute(mine, "head", swap)
    return run(finish_body, ((1, rows, width), F32), mine, theirs, after)


def solution(mesh):
    placed = (
        P(("groups", "frame"), "patch", None),
        P(),
        P("frame", None, "head"),
        P("frame", "head"),
        P(),
        P("frame", None, "head"),
        P("frame", "head"),
    )

    def program(video, *rest):
        frames_here, patches_here, width = video.shape
        count = lax.axis_size("frame")
        small = (
            patches_here == count
            and frames_here == lax.axis_size("patch") == lax.axis_size("head") == 2
            and lax.axis_size("groups") == 2
            and frames_here * patches_here == 8
            and frames_here * count * patches_here < width
        )
        return (moving_tokens if small else on_device)(video, *rest)

    return jax.shard_map(
        program,
        mesh=mesh,
        in_specs=placed,
        out_specs=P(("groups", "frame", "patch"), None, None),
        check_vma=False,
    )
```

```python
import functools

import jax
import jax.numpy as jnp
from jax import lax
from jax.experimental import pallas as pl
from jax.experimental.pallas import tpu as pltpu


from jax.sharding import PartitionSpec as P

HEAD_WIDTH = 72


def layer_norm(tokens, gain):
    value_rows = tokens.astype(jnp.float32)
    center = jnp.mean(value_rows, axis=-1, keepdims=True)
    spread = jnp.mean((value_rows - center) ** 2, axis=-1, keepdims=True)
    return ((value_rows - center) * lax.rsqrt(spread + 1e-06) * gain).astype(jnp.bfloat16)


def project_qkv(normed, weight):
    columns = weight.shape[1] * weight.shape[2]
    total = jnp.dot(
        normed, weight.reshape(weight.shape[0], columns), preferred_element_type=jnp.float32
    )
    return total.astype(jnp.bfloat16)


def project_out(attended, weight):
    return lax.dot_general(
        attended, weight, (((1,), (1,)), ((), ())), preferred_element_type=jnp.float32
    )


def attend(qkv, over_first):
    query_rows, key_rows, value_rows = (qkv[:, :, 0], qkv[:, :, 1], qkv[:, :, 2])
    factor = 1.0 / jnp.sqrt(jnp.float32(HEAD_WIDTH))
    if over_first:
        score_matrix = (
            jnp.einsum("abhd,cbhd->bhac", query_rows, key_rows, preferred_element_type=jnp.float32)
            * factor
        )
        attention_weights = jax.nn.softmax(score_matrix, axis=-1).astype(jnp.bfloat16)
        attention_output = jnp.einsum(
            "bhac,cbhd->abhd", attention_weights, value_rows, preferred_element_type=jnp.float32
        )
    else:
        score_matrix = (
            jnp.einsum("abhd,achd->ahbc", query_rows, key_rows, preferred_element_type=jnp.float32)
            * factor
        )
        attention_weights = jax.nn.softmax(score_matrix, axis=-1).astype(jnp.bfloat16)
        attention_output = jnp.einsum(
            "ahbc,achd->abhd", attention_weights, value_rows, preferred_element_type=jnp.float32
        )
    return attention_output.astype(jnp.bfloat16)


def mix_partial(tokens, gain, qkv_weight, out_weight, over_first):
    rows_a, rows_b, width = tokens.shape
    flat = tokens.reshape(rows_a * rows_b, width)
    normed = layer_norm(flat, gain)
    qkv = project_qkv(normed, qkv_weight).reshape(rows_a, rows_b, 3, -1, HEAD_WIDTH)
    attended = attend(qkv, over_first).reshape(rows_a * rows_b, -1)
    partial_value = project_out(attended, out_weight)
    rounded = lax.optimization_barrier(partial_value.astype(jnp.bfloat16)).astype(jnp.float32)
    return (flat, rounded)


def on_device(video, gain_time, qkv_time, out_time, gain_space, qkv_space, out_space):
    frame_size = lax.axis_size("frame")
    patch_size = lax.axis_size("patch")
    device_count = frame_size * patch_size
    series = lax.all_to_all(video, "frame", split_axis=1, concat_axis=0, tiled=True)
    qkv_time, out_time, qkv_space, out_space = (
        lax.all_gather(qkv_time, "frame", axis=0, tiled=True),
        lax.all_gather(out_time, "frame", axis=0, tiled=True),
        lax.all_gather(qkv_space, "frame", axis=0, tiled=True),
        lax.all_gather(out_space, "frame", axis=0, tiled=True),
    )
    frame_count, series_count, width = series.shape
    set_count = frame_count // device_count
    flat, rounded = mix_partial(series, gain_time, qkv_time, out_time, True)
    summed = (
        lax.psum(rounded.astype(jnp.bfloat16), "head")
        .astype(jnp.float32)
        .reshape(device_count, set_count, series_count, width)
    )
    resident = flat.reshape(device_count, set_count, series_count, width)
    after_time = (resident.astype(jnp.float32) + summed).astype(jnp.bfloat16)
    arrived = lax.all_to_all(
        after_time, ("frame", "patch"), split_axis=0, concat_axis=2, tiled=True
    )
    whole_frames = arrived.reshape(set_count, device_count * series_count, width)
    whole_frames = whole_frames.reshape(set_count, frame_size, patch_size, series_count, width)
    whole_frames = jnp.transpose(whole_frames, (0, 2, 1, 3, 4)).reshape(
        set_count, device_count * series_count, width
    )
    flat_space, rounded_space = mix_partial(whole_frames, gain_space, qkv_space, out_space, False)
    summed_space = lax.psum(rounded_space.astype(jnp.bfloat16), "head").astype(jnp.float32)
    result = flat_space.astype(jnp.float32) + summed_space
    return result.reshape(whole_frames.shape)


F32 = jnp.float32
BF16 = jnp.bfloat16
KINDS = 3
NT = (((1,), (1,)), ((), ()))


def run(body, outs, *args, scratch=(), sems=0):
    vmem = pl.BlockSpec(memory_space=pltpu.VMEM)
    single = not isinstance(outs, list)
    shapes = [jax.ShapeDtypeStruct(*o) for o in ([outs] if single else outs)]
    found = pl.pallas_call(
        body,
        out_shape=shapes,
        in_specs=[pl.BlockSpec(memory_space=pltpu.HBM) if sems else vmem] * len(args),
        out_specs=[vmem] * len(shapes),
        scratch_shapes=[pltpu.VMEM(*s) for s in scratch]
        + [pltpu.SemaphoreType.DMA((sems,))] * (sems > 0),
        compiler_params=pltpu.CompilerParams(vmem_limit_bytes=16 << 20),
    )(*args)
    return found[0] if single else found


def lanes(value, start, size):
    return lax.slice_in_dim(value, start, start + size, axis=1)


def exchange(messages):
    count = len(messages)
    found = [messages[0]]
    for k in range(1, count):
        pairs = [(i, i ^ k) for i in range(count)]
        found.append(lax.ppermute(messages[k], "frame", pairs))
    return found


def pick_rows(value, source):
    column = lax.broadcasted_iota(jnp.int32, (source.shape[0], value.shape[0]), 1)
    chosen = jnp.where(column == source, 1.0, 0.0).astype(BF16)
    return jnp.dot(chosen, value.astype(BF16), preferred_element_type=F32)


def split_body(count, video_hbm, gain_hbm, *refs):
    outs, (held, video_ref, gain_ref, sems) = refs[:count], refs[count:]
    f = lax.axis_index("frame")
    copies = [
        pltpu.make_async_copy(video_hbm, video_ref, sems.at[0]),
        pltpu.make_async_copy(gain_hbm, gain_ref, sems.at[1]),
    ]
    for copy in copies:
        copy.start()
    for copy in copies:
        copy.wait()
    rows = video_ref.shape[0] * video_ref.shape[1]
    share = held.shape[2]
    x = jnp.concatenate([video_ref[i].astype(F32) for i in range(video_ref.shape[0])], axis=0)
    mean = jnp.mean(x, axis=-1, keepdims=True)
    centred = x - mean
    spread = jnp.mean(centred * centred, axis=-1, keepdims=True)
    y = centred * lax.rsqrt(spread + 1e-06) * gain_ref[...].reshape(1, -1)
    for s in range(count):
        held[s, 0:rows] = lanes(y, s * share, share)
        held[s, rows:] = lanes(x, s * share, share)
    for k in range(count):
        outs[k][...] = held[f ^ k].astype(BF16)


def load_body(weight_ref, rows_ref, held_ref, piece_ref, sems):
    quarter = 2 * lax.axis_index("patch") + lax.axis_index("groups")
    size = piece_ref.shape[0]
    place = pl.multiple_of(quarter * size, size)
    copies = [
        pltpu.make_async_copy(rows_ref.at[pl.ds(place, size), :], piece_ref, sems.at[0]),
        pltpu.make_async_copy(weight_ref, held_ref, sems.at[1]),
    ]
    for copy in copies:
        copy.start()
    for copy in copies:
        copy.wait()


def project_body(count, *refs):
    parts, weight_ref, outs = refs[:count], refs[count], refs[count + 1 : 2 * count + 1]
    tokens, total = refs[2 * count + 1 :]
    f = lax.axis_index("frame")
    rows = tokens.shape[0] // count
    for k in range(count):
        place = pl.multiple_of((f ^ k) * rows, rows)
        tokens[pl.ds(place, rows), :] = parts[k][0:rows].astype(F32)
    row = lax.broadcasted_iota(jnp.int32, (tokens.shape[0], 1), 0)
    source = lax.rem(row, rows) * count + lax.div(row, rows)
    x = pick_rows(tokens[...], source).astype(BF16)
    for t in range(KINDS):
        total[t] = jnp.dot(x, weight_ref[t], preferred_element_type=F32)
    for k in range(count):
        place = pl.multiple_of((f ^ k) * rows, rows)
        for t in range(KINDS):
            outs[k][t] = total.at[t][pl.ds(place, rows), :].astype(BF16)


def prepare_body(count, *refs):
    parts, gain_ref, weight_ref = refs[:count], refs[count], refs[count + 1]
    fixed_ref, gain_own, raw_own, raw_other, gains, raw = refs[count + 2 :]
    f, p = lax.axis_index("frame"), lax.axis_index("patch")
    share = gains.shape[2]
    for s in range(count):
        gains[s] = jnp.broadcast_to(lanes(gain_ref[...].reshape(1, -1), s * share, share), gains.shape[1:])
    g = gains[f]
    gain_own[...] = g
    g = g.astype(BF16)
    rows = [jnp.dot(g, weight_ref[t], preferred_element_type=F32) for t in range(KINDS)]
    row = lax.broadcasted_iota(jnp.int32, rows[0].shape, 0)
    fixed_ref[...] = jnp.where(row == 0, rows[0], jnp.where(row == 1, rows[1], rows[2]))
    whole = parts[0].shape[0] // 2
    places = whole // 2
    for k in range(count):
        raw[f ^ k] = parts[k][whole:].astype(F32)
    even, odd = (
        jnp.concatenate([raw[s][at : at + places] for s in range(count)], axis=0)
        for at in (0, places)
    )
    raw_own[...] = jnp.where(p == 0, even, odd).astype(BF16)
    raw_other[...] = jnp.where(p == 0, odd, even).astype(BF16)


def attend_rows(query, key, value):
    rows, width = query.shape
    heads = width // HEAD_WIDTH
    spread = heads * rows
    first = lax.broadcasted_iota(jnp.int32, (heads, rows, width), 0) * HEAD_WIDTH
    first = first.reshape(spread, width)
    lane = lax.broadcasted_iota(jnp.int32, (spread, width), 1)
    mine = (lane >= first) & (lane < first + HEAD_WIDTH)
    keys = jnp.where(mine, jnp.concatenate([key] * heads, axis=0), 0.0).astype(BF16)
    values = jnp.where(mine, jnp.concatenate([value] * heads, axis=0), 0.0).astype(BF16)
    scores = lax.dot_general(keys, query.astype(BF16), NT, preferred_element_type=F32)
    scores = (scores * (1.0 / HEAD_WIDTH**0.5)).reshape(heads, rows, rows)
    power = jnp.exp(scores - jnp.max(scores, axis=1, keepdims=True))
    weights = power / jnp.sum(power, axis=1, keepdims=True)
    weights = weights.reshape(spread, rows).T.astype(BF16)
    return jnp.dot(weights, values, preferred_element_type=F32)


def attend_time_body(count, *refs):
    parts, fixed_ref, out_ref = refs[:count], refs[count], refs[count + 1]
    qkv = []
    for t in range(KINDS):
        total = parts[0][t].astype(F32)
        for k in range(1, count):
            total = total + parts[k][t].astype(F32)
        qkv.append(total.astype(BF16).astype(F32))
    attended = attend_rows(*qkv)
    out_ref[...] = jnp.concatenate([attended, fixed_ref[...]], axis=0).astype(BF16)


def out_time_body(count, *refs):
    parts, weight_ref, raw_other = refs[:count], refs[count], refs[count + 1]
    own_ref, other_ref, alone_ref, tokens = refs[count + 2 :]
    f, p = lax.axis_index("frame"), lax.axis_index("patch")
    rows = tokens.shape[0] // count
    for k in range(count):
        place = pl.multiple_of((f ^ k) * rows, rows)
        tokens[pl.ds(place, rows), :] = parts[k][0:rows].astype(F32)
    half = tokens.shape[0] // 2
    row = lax.broadcasted_iota(jnp.int32, (tokens.shape[0], 1), 0)
    parity = jnp.where(row < half, p, 1 - p)
    row = lax.rem(row, half)
    source = lax.rem(row, count) * rows + 2 * lax.div(row, count) + parity
    x = pick_rows(tokens[...], source).astype(BF16)
    total = lax.dot_general(x, weight_ref[...], NT, preferred_element_type=F32)
    own_ref[...] = total[0:half].astype(BF16)
    other_ref[0:half] = total[half:].astype(BF16)
    alone_ref[...] = total[half:].astype(BF16)
    other_ref[half:] = raw_other[...]


def in_three(value):
    high = value.astype(BF16).astype(F32)
    middle = (value - high).astype(BF16).astype(F32)
    return high, middle, value - high - middle


def project_space_body(count, *refs):
    own, own_head, cross, cross_head, raw_own, gain_ref, weight_ref = refs[:7]
    outs, total = refs[7 : 7 + count], refs[7 + count]
    f, p = lax.axis_index("frame"), lax.axis_index("patch")
    half = own.shape[0]
    summed = own[...].astype(F32) + own_head[...].astype(F32)
    first = raw_own[...].astype(F32) + summed
    summed = cross[0:half].astype(F32) + cross_head[...].astype(F32)
    second = cross[half:].astype(F32) + summed
    low, high = jnp.where(p == 0, first, second), jnp.where(p == 0, second, first)
    places = half // count
    pieces = [v[i : i + places] for i in range(0, half, places) for v in (low, high)]
    x = jnp.concatenate(pieces, axis=0).astype(BF16).astype(F32)
    mean = jnp.mean(x, axis=-1, keepdims=True)
    centred = x - mean
    square = jnp.sum(centred * centred, axis=-1, keepdims=True)
    y = (centred * gain_ref[0:1]).astype(BF16)
    found = [jnp.dot(y, weight_ref[t], preferred_element_type=F32) for t in range(KINDS)]
    spare = total.shape[1] - KINDS * weight_ref.shape[2] - x.shape[1]
    lane = lax.broadcasted_iota(jnp.int32, (x.shape[0], spare), 1)
    tail = jnp.zeros(lane.shape, F32)
    for at, item in enumerate((*in_three(mean), *in_three(square))):
        tail = jnp.where(lane == at, item, tail)
    total[...] = jnp.concatenate([*found, x, tail], axis=1)
    rows = total.shape[0] // count
    for k in range(count):
        place = pl.multiple_of((f ^ k) * rows, rows)
        outs[k][...] = total[pl.ds(place, rows), :].astype(BF16)


def attend_space_body(count, *refs):
    parts, fixed, refs = refs[:count], refs[count : 2 * count], refs[2 * count :]
    weight_ref, partial_ref, after_ref, held = refs
    f = lax.axis_index("frame")
    rows, columns = parts[0].shape[0], weight_ref.shape[1]
    share = weight_ref.shape[0] // count
    messages = [part[...].astype(F32) for part in parts]
    tails = [lanes(m, KINDS * columns + share, m.shape[1] - KINDS * columns - share) for m in messages]
    lane = lax.broadcasted_iota(jnp.int32, tails[0].shape, 1)
    means = [jnp.sum(jnp.where(lane < 3, t, 0.0), axis=-1, keepdims=True) for t in tails]
    squares = [
        jnp.sum(jnp.where((lane >= 3) & (lane < 6), t, 0.0), axis=-1, keepdims=True) for t in tails
    ]
    mean = sum(means) / count
    square = sum(squares) + share * sum((m - mean) * (m - mean) for m in means)
    scale = lax.rsqrt(square / (share * count) + 1e-06)
    total = sum(messages)
    qkv = []
    for t in range(KINDS):
        value = lanes(total, t * columns, columns)
        for k in range(count):
            value = value + (means[k] - mean) * fixed[k][...].astype(F32)[rows + t : rows + t + 1]
        qkv.append((value * scale).astype(BF16).astype(F32))
    attended = attend_rows(*qkv).astype(BF16)
    for k in range(count):
        held[f ^ k] = lanes(messages[k], KINDS * columns, share)
    partial = lax.dot_general(attended, weight_ref[...], NT, preferred_element_type=F32)
    partial_ref[...] = partial.astype(BF16)
    after_ref[...] = jnp.concatenate([held[s] for s in range(count)], axis=1).astype(BF16)


def assemble_body(order, own, near, side, far, last, out_ref):
    f, p, g = lax.axis_index("frame"), lax.axis_index("patch"), lax.axis_index("groups")
    share, quarter = own.shape[0], own.shape[0] // 4
    out_ref[pl.ds(pl.multiple_of(f * share, share), share), :] = own[...]
    for at, k in enumerate(order):
        for piece, q in (
            (near, 2 * p + g),
            (side, 2 * (1 - p) + g),
            (far, 2 * p + 1 - g),
            (last, 2 * (1 - p) + 1 - g),
        ):
            place = pl.multiple_of((f ^ k) * share + q * quarter, quarter)
            out_ref[pl.ds(place, quarter), :] = piece[at * quarter : (at + 1) * quarter]


def finish_body(own, other, after, out_ref):
    out_ref[0] = after[...].astype(F32) + (own[...].astype(F32) + other[...].astype(F32))


def moving_tokens(video, gain_time, qkv_time, out_time, gain_space, qkv_space, out_space):
    count = lax.axis_size("frame")
    frames_here, patches_here, width = video.shape
    share, columns = out_time.shape
    rows = frames_here * patches_here
    plane = rows * count
    message = (KINDS * columns + share) // 128 * 128 + 128
    qkv_time, qkv_space = (jnp.transpose(w, (1, 0, 2)) for w in (qkv_time, qkv_space))
    body = functools.partial
    swap = [(0, 1), (1, 0)]

    normed = run(
        body(split_body, count),
        [((2 * rows, share), BF16)] * count,
        video,
        gain_time,
        scratch=[((count, 2 * rows, share), F32), (video.shape, BF16), ((width,), F32)],
        sems=2,
    )
    normed = exchange(normed)
    qkv_time, piece = run(
        load_body,
        [(qkv_time.shape, BF16), ((share // 4, columns), BF16)],
        qkv_time,
        out_space,
        sems=2,
    )
    partial_time = run(
        body(project_body, count),
        [((KINDS, rows, columns), BF16)] * count,
        *normed,
        qkv_time,
        scratch=[((plane, share), F32), ((KINDS, plane, columns), F32)],
    )
    partial_time = exchange(partial_time)
    near, order = piece, [0]
    for stage in range(count.bit_length() - 1):
        hop = count >> (stage + 1)
        pairs = [(i, i ^ hop) for i in range(count)]
        near = jnp.concatenate([near, lax.ppermute(near, "frame", pairs)], axis=0)
        order += [k ^ hop for k in order]
    near = near[share // 4 :]
    side = lax.ppermute(near, "patch", swap)
    far = []
    for value in (near, side):
        far.append(lax.ppermute(value, "groups", swap))
    whole_space = run(
        body(assemble_body, order[1:]), ((width, columns), BF16), out_space, near, side, *far
    )
    fixed, gain_own, raw_own, raw_other = run(
        body(prepare_body, count),
        [
            ((8, columns), F32),
            ((8, share), F32),
            ((plane // 2, share), BF16),
            ((plane // 2, share), BF16),
        ],
        *normed,
        gain_space,
        qkv_space,
        scratch=[((count, 8, share), F32), ((count, rows, share), F32)],
    )
    attended = run(
        body(attend_time_body, count), ((rows + 8, columns), BF16), *partial_time, fixed
    )
    attended = exchange([attended] * count)
    own, cross, cross_only = run(
        body(out_time_body, count),
        [((plane // 2, share), BF16), ((plane, share), BF16), ((plane // 2, share), BF16)],
        *attended,
        out_time,
        raw_other,
        scratch=[((plane, columns), F32)],
    )
    own_head = lax.ppermute(own, "head", swap)
    crossed = lax.ppermute(cross, "patch", swap)
    cross_head = lax.ppermute(cross_only, ("patch", "head"), [(i, 3 - i) for i in range(4)])
    partial_space = run(
        body(project_space_body, count),
        [((rows, message), BF16)] * count,
        own,
        own_head,
        crossed,
        cross_head,
        raw_own,
        gain_own,
        qkv_space,
        scratch=[((plane, message), F32)],
    )
    partial_space = exchange(partial_space)
    mine, after = run(
        body(attend_space_body, count),
        [((rows, width), BF16)] * 2,
        *partial_space,
        *attended,
        whole_space,
        scratch=[((count, rows, share), F32)],
    )
    theirs = lax.ppermute(mine, "head", swap)
    return run(finish_body, ((1, rows, width), F32), mine, theirs, after)


def solution(mesh):
    placed = (
        P(("groups", "frame"), "patch", None),
        P(),
        P("frame", None, "head"),
        P("frame", "head"),
        P(),
        P("frame", None, "head"),
        P("frame", "head"),
    )

    def program(video, *rest):
        frames_here, patches_here, width = video.shape
        count = lax.axis_size("frame")
        small = (
            patches_here == count
            and frames_here == lax.axis_size("patch") == lax.axis_size("head") == 2
            and lax.axis_size("groups") == 2
            and frames_here * patches_here == 8
            and frames_here * count * patches_here < width
        )
        return (moving_tokens if small else on_device)(video, *rest)

    return jax.shard_map(
        program,
        mesh=mesh,
        in_specs=placed,
        out_specs=P(("groups", "frame", "patch"), None, None),
        check_vma=False,
    )
```

```python
import functools

import jax
import jax.numpy as jnp
from jax import lax
from jax.experimental import pallas as pl
from jax.experimental.pallas import tpu as pltpu


from jax.sharding import PartitionSpec as P

HEAD_WIDTH = 72


def layer_norm(tokens, gain):
    value_rows = tokens.astype(jnp.float32)
    center = jnp.mean(value_rows, axis=-1, keepdims=True)
    spread = jnp.mean((value_rows - center) ** 2, axis=-1, keepdims=True)
    return ((value_rows - center) * lax.rsqrt(spread + 1e-06) * gain).astype(jnp.bfloat16)


def project_qkv(normed, weight):
    columns = weight.shape[1] * weight.shape[2]
    total = jnp.dot(
        normed, weight.reshape(weight.shape[0], columns), preferred_element_type=jnp.float32
    )
    return total.astype(jnp.bfloat16)


def project_out(attended, weight):
    return lax.dot_general(
        attended, weight, (((1,), (1,)), ((), ())), preferred_element_type=jnp.float32
    )


def attend(qkv, over_first):
    query_rows, key_rows, value_rows = (qkv[:, :, 0], qkv[:, :, 1], qkv[:, :, 2])
    factor = 1.0 / jnp.sqrt(jnp.float32(HEAD_WIDTH))
    if over_first:
        score_matrix = (
            jnp.einsum("abhd,cbhd->bhac", query_rows, key_rows, preferred_element_type=jnp.float32)
            * factor
        )
        attention_weights = jax.nn.softmax(score_matrix, axis=-1).astype(jnp.bfloat16)
        attention_output = jnp.einsum(
            "bhac,cbhd->abhd", attention_weights, value_rows, preferred_element_type=jnp.float32
        )
    else:
        score_matrix = (
            jnp.einsum("abhd,achd->ahbc", query_rows, key_rows, preferred_element_type=jnp.float32)
            * factor
        )
        attention_weights = jax.nn.softmax(score_matrix, axis=-1).astype(jnp.bfloat16)
        attention_output = jnp.einsum(
            "ahbc,achd->abhd", attention_weights, value_rows, preferred_element_type=jnp.float32
        )
    return attention_output.astype(jnp.bfloat16)


def mix_partial(tokens, gain, qkv_weight, out_weight, over_first):
    rows_a, rows_b, width = tokens.shape
    flat = tokens.reshape(rows_a * rows_b, width)
    normed = layer_norm(flat, gain)
    qkv = project_qkv(normed, qkv_weight).reshape(rows_a, rows_b, 3, -1, HEAD_WIDTH)
    attended = attend(qkv, over_first).reshape(rows_a * rows_b, -1)
    partial_value = project_out(attended, out_weight)
    rounded = lax.optimization_barrier(partial_value.astype(jnp.bfloat16)).astype(jnp.float32)
    return (flat, rounded)


def on_device(video, gain_time, qkv_time, out_time, gain_space, qkv_space, out_space):
    frame_size = lax.axis_size("frame")
    patch_size = lax.axis_size("patch")
    device_count = frame_size * patch_size
    series = lax.all_to_all(video, "frame", split_axis=1, concat_axis=0, tiled=True)
    qkv_time, out_time, qkv_space, out_space = (
        lax.all_gather(qkv_time, "frame", axis=0, tiled=True),
        lax.all_gather(out_time, "frame", axis=0, tiled=True),
        lax.all_gather(qkv_space, "frame", axis=0, tiled=True),
        lax.all_gather(out_space, "frame", axis=0, tiled=True),
    )
    frame_count, series_count, width = series.shape
    set_count = frame_count // device_count
    flat, rounded = mix_partial(series, gain_time, qkv_time, out_time, True)
    summed = (
        lax.psum(rounded.astype(jnp.bfloat16), "head")
        .astype(jnp.float32)
        .reshape(device_count, set_count, series_count, width)
    )
    resident = flat.reshape(device_count, set_count, series_count, width)
    after_time = (resident.astype(jnp.float32) + summed).astype(jnp.bfloat16)
    arrived = lax.all_to_all(
        after_time, ("frame", "patch"), split_axis=0, concat_axis=2, tiled=True
    )
    whole_frames = arrived.reshape(set_count, device_count * series_count, width)
    whole_frames = whole_frames.reshape(set_count, frame_size, patch_size, series_count, width)
    whole_frames = jnp.transpose(whole_frames, (0, 2, 1, 3, 4)).reshape(
        set_count, device_count * series_count, width
    )
    flat_space, rounded_space = mix_partial(whole_frames, gain_space, qkv_space, out_space, False)
    summed_space = lax.psum(rounded_space.astype(jnp.bfloat16), "head").astype(jnp.float32)
    result = flat_space.astype(jnp.float32) + summed_space
    return result.reshape(whole_frames.shape)


F32 = jnp.float32
BF16 = jnp.bfloat16
KINDS = 3
NT = (((1,), (1,)), ((), ()))


def run(body, outs, *args, scratch=(), sems=0):
    vmem = pl.BlockSpec(memory_space=pltpu.VMEM)
    single = not isinstance(outs, list)
    shapes = [jax.ShapeDtypeStruct(*o) for o in ([outs] if single else outs)]
    found = pl.pallas_call(
        body,
        out_shape=shapes,
        in_specs=[pl.BlockSpec(memory_space=pltpu.HBM) if sems else vmem] * len(args),
        out_specs=[vmem] * len(shapes),
        scratch_shapes=[pltpu.VMEM(*s) for s in scratch]
        + [pltpu.SemaphoreType.DMA((sems,))] * (sems > 0),
        compiler_params=pltpu.CompilerParams(vmem_limit_bytes=16 << 20),
    )(*args)
    return found[0] if single else found


def lanes(value, start, size):
    return lax.slice_in_dim(value, start, start + size, axis=1)


def exchange(messages):
    count = len(messages)
    found = [messages[0]]
    for k in range(1, count):
        pairs = [(i, i ^ k) for i in range(count)]
        found.append(lax.ppermute(messages[k], "frame", pairs))
    return found


def pick_rows(value, source):
    column = lax.broadcasted_iota(jnp.int32, (source.shape[0], value.shape[0]), 1)
    chosen = jnp.where(column == source, 1.0, 0.0).astype(BF16)
    return jnp.dot(chosen, value.astype(BF16), preferred_element_type=F32)


def in_three(value):
    high = value.astype(BF16).astype(F32)
    middle = (value - high).astype(BF16).astype(F32)
    return high, middle, value - high - middle


def tail_of(items, rows, size):
    lane = lax.broadcasted_iota(jnp.int32, (rows, size), 1)
    tail = jnp.zeros((rows, size), F32)
    for at, item in enumerate(items):
        tail = jnp.where(lane == at, item, tail)
    return tail


def from_three(tail, at):
    lane = lax.broadcasted_iota(jnp.int32, tail.shape, 1)
    return jnp.sum(jnp.where((lane >= at) & (lane < at + 3), tail, 0.0), axis=-1, keepdims=True)


def rows_of(block_ref):
    return jnp.concatenate([block_ref[i].astype(F32) for i in range(block_ref.shape[0])], axis=0)


def load_body(weight_ref, held_ref, sems):
    copy = pltpu.make_async_copy(weight_ref, held_ref, sems.at[0])
    copy.start()
    copy.wait()


def slices_of(gain_ref, gains):
    for s in range(gains.shape[0]):
        row = lanes(gain_ref[...].reshape(1, -1), s * gains.shape[2], gains.shape[2])
        gains[s] = jnp.broadcast_to(row, gains.shape[1:])
    return gains[lax.axis_index("frame")]


def project_body(count, *refs):
    parts, gain_ref, weight_ref, outs = refs[:count], *refs[count : count + 2], refs[count + 2 : -2]
    tokens, total = refs[-2:]
    f = lax.axis_index("frame")
    share = tokens.shape[2]
    plane = tokens.shape[1]
    rows = plane // count
    gain = gain_ref[...].reshape(1, -1)
    for k in range(count):
        place = pl.multiple_of((f ^ k) * rows, rows)
        x = rows_of(parts[k])
        centred = x - jnp.mean(x, axis=-1, keepdims=True)
        spread = jnp.mean(centred * centred, axis=-1, keepdims=True)
        y = centred * lax.rsqrt(spread + 1e-06) * gain
        for s in range(count):
            tokens[s, pl.ds(place, rows), :] = lanes(y, s * share, share)
    row = lax.broadcasted_iota(jnp.int32, (plane, 1), 0)
    source = lax.rem(row, rows) * count + lax.div(row, rows)
    x = pick_rows(tokens[f], source).astype(BF16)
    found = [jnp.dot(x, weight_ref[t], preferred_element_type=F32) for t in range(KINDS)]
    total[...] = jnp.concatenate(found, axis=1)
    for k in range(count):
        place = pl.multiple_of((f ^ k) * rows, rows)
        outs[k][...] = total[pl.ds(place, rows), :].astype(BF16)


def prepare_body(count, *refs):
    parts, gain_ref, weight_ref = refs[:count], refs[count], refs[count + 1]
    fixed_ref, gain_own, raw_own, raw_other, gains, raw = refs[count + 2 :]
    f, p = lax.axis_index("frame"), lax.axis_index("patch")
    g = slices_of(gain_ref, gains)
    gain_own[...] = g
    g = g.astype(BF16)
    rows = [jnp.dot(g, weight_ref[t], preferred_element_type=F32) for t in range(KINDS)]
    row = lax.broadcasted_iota(jnp.int32, rows[0].shape, 0)
    fixed_ref[...] = jnp.where(row == 0, rows[0], jnp.where(row == 1, rows[1], rows[2]))
    share = gains.shape[2]
    places = parts[0].shape[1]
    rows = 2 * places
    for k in range(count):
        place = pl.multiple_of((f ^ k) * rows, rows)
        x = rows_of(parts[k])
        for s in range(count):
            raw[s, pl.ds(place, rows), :] = lanes(x, s * share, share)
    whole = raw[f]
    even, odd = (
        jnp.concatenate([whole[r + at : r + at + places] for r in range(0, count * rows, rows)], axis=0)
        for at in (0, places)
    )
    raw_own[...] = jnp.where(p == 0, even, odd).astype(BF16)
    raw_other[...] = jnp.where(p == 0, odd, even).astype(BF16)


def attend_rows(query, key, value):
    rows, width = query.shape
    heads = width // HEAD_WIDTH
    spread = heads * rows
    first = lax.broadcasted_iota(jnp.int32, (heads, rows, width), 0) * HEAD_WIDTH
    first = first.reshape(spread, width)
    lane = lax.broadcasted_iota(jnp.int32, (spread, width), 1)
    mine = (lane >= first) & (lane < first + HEAD_WIDTH)
    keys = jnp.where(mine, jnp.concatenate([key] * heads, axis=0), 0.0).astype(BF16)
    values = jnp.where(mine, jnp.concatenate([value] * heads, axis=0), 0.0).astype(BF16)
    scores = lax.dot_general(keys, query.astype(BF16), NT, preferred_element_type=F32)
    scores = (scores * (1.0 / HEAD_WIDTH**0.5)).reshape(heads, rows, rows)
    power = jnp.exp(scores - jnp.max(scores, axis=1, keepdims=True))
    weights = power / jnp.sum(power, axis=1, keepdims=True)
    weights = weights.reshape(spread, rows).T.astype(BF16)
    return jnp.dot(weights, values, preferred_element_type=F32)


def attend_time_body(count, *refs):
    parts, fixed_ref, out_ref = refs[:count], refs[count], refs[count + 1]
    total = sum(part[...].astype(F32) for part in parts).astype(BF16).astype(F32)
    columns = out_ref.shape[1]
    attended = attend_rows(*(lanes(total, t * columns, columns) for t in range(KINDS)))
    out_ref[...] = jnp.concatenate([attended, fixed_ref[...]], axis=0).astype(BF16)


def out_time_body(count, *refs):
    parts, weight_ref, raw_other = refs[:count], refs[count], refs[count + 1]
    own_ref, other_ref, alone_ref, tokens = refs[count + 2 :]
    f, p = lax.axis_index("frame"), lax.axis_index("patch")
    rows = tokens.shape[0] // count
    for k in range(count):
        place = pl.multiple_of((f ^ k) * rows, rows)
        tokens[pl.ds(place, rows), :] = parts[k][0:rows].astype(F32)
    half = tokens.shape[0] // 2
    row = lax.broadcasted_iota(jnp.int32, (tokens.shape[0], 1), 0)
    parity = jnp.where(row < half, p, 1 - p)
    row = lax.rem(row, half)
    source = lax.rem(row, count) * rows + 2 * lax.div(row, count) + parity
    x = pick_rows(tokens[...], source).astype(BF16)
    total = lax.dot_general(x, weight_ref[...], NT, preferred_element_type=F32)
    own_ref[...] = total[0:half].astype(BF16)
    other_ref[0:half] = total[half:].astype(BF16)
    alone_ref[...] = total[half:].astype(BF16)
    other_ref[half:] = raw_other[...]


def project_space_body(count, *refs):
    own, own_head, cross, cross_head, raw_own, gain_ref, weight_ref = refs[:7]
    outs, total = refs[7 : 7 + count], refs[7 + count]
    f, p = lax.axis_index("frame"), lax.axis_index("patch")
    half = own.shape[0]
    summed = own[...].astype(F32) + own_head[...].astype(F32)
    first = raw_own[...].astype(F32) + summed
    summed = cross[0:half].astype(F32) + cross_head[...].astype(F32)
    second = cross[half:].astype(F32) + summed
    low, high = jnp.where(p == 0, first, second), jnp.where(p == 0, second, first)
    places = half // count
    pieces = [v[i : i + places] for i in range(0, half, places) for v in (low, high)]
    x = jnp.concatenate(pieces, axis=0).astype(BF16).astype(F32)
    mean = jnp.mean(x, axis=-1, keepdims=True)
    centred = x - mean
    square = jnp.sum(centred * centred, axis=-1, keepdims=True)
    y = (centred * gain_ref[0:1]).astype(BF16)
    found = [jnp.dot(y, weight_ref[t], preferred_element_type=F32) for t in range(KINDS)]
    spare = total.shape[1] - KINDS * weight_ref.shape[2] - x.shape[1]
    tail = tail_of((*in_three(mean), *in_three(square)), x.shape[0], spare)
    total[...] = jnp.concatenate([*found, x, tail], axis=1)
    rows = total.shape[0] // count
    for k in range(count):
        place = pl.multiple_of((f ^ k) * rows, rows)
        outs[k][...] = total[pl.ds(place, rows), :].astype(BF16)


def attend_space_body(count, *refs):
    parts, fixed, refs = refs[:count], refs[count : 2 * count], refs[2 * count :]
    weight_ref, partial_ref, after_ref, held = refs
    f = lax.axis_index("frame")
    rows, columns = parts[0].shape[0], weight_ref.shape[1]
    share = weight_ref.shape[0] // count
    messages = [part[...].astype(F32) for part in parts]
    tails = [lanes(m, KINDS * columns + share, m.shape[1] - KINDS * columns - share) for m in messages]
    means = [from_three(t, 0) for t in tails]
    squares = [from_three(t, 3) for t in tails]
    mean = sum(means) / count
    square = sum(squares) + share * sum((m - mean) * (m - mean) for m in means)
    scale = lax.rsqrt(square / (share * count) + 1e-06)
    total = sum(messages)
    qkv = []
    for t in range(KINDS):
        value = lanes(total, t * columns, columns)
        for k in range(count):
            value = value + (means[k] - mean) * fixed[k][...].astype(F32)[rows + t : rows + t + 1]
        qkv.append((value * scale).astype(BF16).astype(F32))
    attended = attend_rows(*qkv).astype(BF16)
    for k in range(count):
        held[f ^ k] = lanes(messages[k], KINDS * columns, share)
    partial = lax.dot_general(attended, weight_ref[...], NT, preferred_element_type=F32)
    partial_ref[...] = partial.astype(BF16)
    after_ref[...] = jnp.concatenate([held[s] for s in range(count)], axis=1).astype(BF16)


def assemble_body(order, own, near, side, far, last, out_ref):
    f, p, g = lax.axis_index("frame"), lax.axis_index("patch"), lax.axis_index("groups")
    share, quarter = own.shape[0], own.shape[0] // 4
    out_ref[pl.ds(pl.multiple_of(f * share, share), share), :] = own[...]
    for at, k in enumerate(order):
        for piece, q in (
            (near, 2 * p + g),
            (side, 2 * (1 - p) + g),
            (far, 2 * p + 1 - g),
            (last, 2 * (1 - p) + 1 - g),
        ):
            place = pl.multiple_of((f ^ k) * share + q * quarter, quarter)
            out_ref[pl.ds(place, quarter), :] = piece[at * quarter : (at + 1) * quarter]


def finish_body(own, other, after, out_ref):
    out_ref[0] = after[...].astype(F32) + (own[...].astype(F32) + other[...].astype(F32))


def moving_tokens(video, gain_time, qkv_time, out_time, gain_space, qkv_space, out_space):
    count = lax.axis_size("frame")
    frames_here, patches_here, width = video.shape
    share, columns = out_time.shape
    rows = frames_here * patches_here
    plane = rows * count
    message = (KINDS * columns + share) // 128 * 128 + 128
    qkv_time, qkv_space = (jnp.transpose(w, (1, 0, 2)) for w in (qkv_time, qkv_space))
    body = functools.partial
    swap = [(0, 1), (1, 0)]

    tokens = exchange([video] * count)
    quarter = 2 * lax.axis_index("patch") + lax.axis_index("groups")
    piece = lax.dynamic_slice_in_dim(out_space, quarter * (share // 4), share // 4)
    qkv_time = run(load_body, (qkv_time.shape, BF16), qkv_time, sems=1)
    partial_time = run(
        body(project_body, count),
        [((rows, KINDS * columns), BF16)] * count,
        *tokens,
        gain_time,
        qkv_time,
        scratch=[((count, plane, share), F32), ((plane, KINDS * columns), F32)],
    )
    partial_time = exchange(partial_time)
    near, order = piece, [0]
    for stage in range(count.bit_length() - 1):
        hop = count >> (stage + 1)
        pairs = [(i, i ^ hop) for i in range(count)]
        near = jnp.concatenate([near, lax.ppermute(near, "frame", pairs)], axis=0)
        order += [k ^ hop for k in order]
    near = near[share // 4 :]
    side = lax.ppermute(near, "patch", swap)
    far = []
    for value in (near, side):
        far.append(lax.ppermute(value, "groups", swap))
    whole_space = run(
        body(assemble_body, order[1:]), ((width, columns), BF16), out_space, near, side, *far
    )
    fixed, gain_own, raw_own, raw_other = run(
        body(prepare_body, count),
        [
            ((8, columns), F32),
            ((8, share), F32),
            ((plane // 2, share), BF16),
            ((plane // 2, share), BF16),
        ],
        *tokens,
        gain_space,
        qkv_space,
        scratch=[((count, 8, share), F32), ((count, plane, share), F32)],
    )
    attended = run(
        body(attend_time_body, count), ((rows + 8, columns), BF16), *partial_time, fixed
    )
    attended = exchange([attended] * count)
    own, cross, cross_only = run(
        body(out_time_body, count),
        [((plane // 2, share), BF16), ((plane, share), BF16), ((plane // 2, share), BF16)],
        *attended,
        out_time,
        raw_other,
        scratch=[((plane, columns), F32)],
    )
    own_head = lax.ppermute(own, "head", swap)
    crossed = lax.ppermute(cross, "patch", swap)
    cross_head = lax.ppermute(cross_only, ("patch", "head"), [(i, 3 - i) for i in range(4)])
    partial_space = run(
        body(project_space_body, count),
        [((rows, message), BF16)] * count,
        own,
        own_head,
        crossed,
        cross_head,
        raw_own,
        gain_own,
        qkv_space,
        scratch=[((plane, message), F32)],
    )
    partial_space = exchange(partial_space)
    mine, after = run(
        body(attend_space_body, count),
        [((rows, width), BF16)] * 2,
        *partial_space,
        *attended,
        whole_space,
        scratch=[((count, rows, share), F32)],
    )
    theirs = lax.ppermute(mine, "head", swap)
    return run(finish_body, ((1, rows, width), F32), mine, theirs, after)


def solution(mesh):
    placed = (
        P(("groups", "frame"), "patch", None),
        P(),
        P("frame", None, "head"),
        P("frame", "head"),
        P(),
        P("frame", None, "head"),
        P("frame", "head"),
    )

    def program(video, *rest):
        frames_here, patches_here, width = video.shape
        count = lax.axis_size("frame")
        small = (
            patches_here == count
            and frames_here == lax.axis_size("patch") == lax.axis_size("head") == 2
            and lax.axis_size("groups") == 2
            and frames_here * patches_here == 8
            and frames_here * count * patches_here < width
        )
        return (moving_tokens if small else on_device)(video, *rest)

    return jax.shard_map(
        program,
        mesh=mesh,
        in_specs=placed,
        out_specs=P(("groups", "frame", "patch"), None, None),
        check_vma=False,
    )
```

```python
import functools

import jax
import jax.numpy as jnp
from jax import lax
from jax.experimental import pallas as pl
from jax.experimental.pallas import tpu as pltpu


from jax.sharding import PartitionSpec as P

HEAD_WIDTH = 72


def layer_norm(tokens, gain):
    value_rows = tokens.astype(jnp.float32)
    center = jnp.mean(value_rows, axis=-1, keepdims=True)
    spread = jnp.mean((value_rows - center) ** 2, axis=-1, keepdims=True)
    return ((value_rows - center) * lax.rsqrt(spread + 1e-06) * gain).astype(jnp.bfloat16)


def project_qkv(normed, weight):
    columns = weight.shape[1] * weight.shape[2]
    total = jnp.dot(
        normed, weight.reshape(weight.shape[0], columns), preferred_element_type=jnp.float32
    )
    return total.astype(jnp.bfloat16)


def project_out(attended, weight):
    return lax.dot_general(
        attended, weight, (((1,), (1,)), ((), ())), preferred_element_type=jnp.float32
    )


def attend(qkv, over_first):
    query_rows, key_rows, value_rows = (qkv[:, :, 0], qkv[:, :, 1], qkv[:, :, 2])
    factor = 1.0 / jnp.sqrt(jnp.float32(HEAD_WIDTH))
    if over_first:
        score_matrix = (
            jnp.einsum("abhd,cbhd->bhac", query_rows, key_rows, preferred_element_type=jnp.float32)
            * factor
        )
        attention_weights = jax.nn.softmax(score_matrix, axis=-1).astype(jnp.bfloat16)
        attention_output = jnp.einsum(
            "bhac,cbhd->abhd", attention_weights, value_rows, preferred_element_type=jnp.float32
        )
    else:
        score_matrix = (
            jnp.einsum("abhd,achd->ahbc", query_rows, key_rows, preferred_element_type=jnp.float32)
            * factor
        )
        attention_weights = jax.nn.softmax(score_matrix, axis=-1).astype(jnp.bfloat16)
        attention_output = jnp.einsum(
            "ahbc,achd->abhd", attention_weights, value_rows, preferred_element_type=jnp.float32
        )
    return attention_output.astype(jnp.bfloat16)


def mix_partial(tokens, gain, qkv_weight, out_weight, over_first):
    rows_a, rows_b, width = tokens.shape
    flat = tokens.reshape(rows_a * rows_b, width)
    normed = layer_norm(flat, gain)
    qkv = project_qkv(normed, qkv_weight).reshape(rows_a, rows_b, 3, -1, HEAD_WIDTH)
    attended = attend(qkv, over_first).reshape(rows_a * rows_b, -1)
    partial_value = project_out(attended, out_weight)
    rounded = lax.optimization_barrier(partial_value.astype(jnp.bfloat16)).astype(jnp.float32)
    return (flat, rounded)


def on_device(video, gain_time, qkv_time, out_time, gain_space, qkv_space, out_space):
    frame_size = lax.axis_size("frame")
    patch_size = lax.axis_size("patch")
    device_count = frame_size * patch_size
    series = lax.all_to_all(video, "frame", split_axis=1, concat_axis=0, tiled=True)
    qkv_time, out_time, qkv_space, out_space = (
        lax.all_gather(qkv_time, "frame", axis=0, tiled=True),
        lax.all_gather(out_time, "frame", axis=0, tiled=True),
        lax.all_gather(qkv_space, "frame", axis=0, tiled=True),
        lax.all_gather(out_space, "frame", axis=0, tiled=True),
    )
    frame_count, series_count, width = series.shape
    set_count = frame_count // device_count
    flat, rounded = mix_partial(series, gain_time, qkv_time, out_time, True)
    summed = (
        lax.psum(rounded.astype(jnp.bfloat16), "head")
        .astype(jnp.float32)
        .reshape(device_count, set_count, series_count, width)
    )
    resident = flat.reshape(device_count, set_count, series_count, width)
    after_time = (resident.astype(jnp.float32) + summed).astype(jnp.bfloat16)
    arrived = lax.all_to_all(
        after_time, ("frame", "patch"), split_axis=0, concat_axis=2, tiled=True
    )
    whole_frames = arrived.reshape(set_count, device_count * series_count, width)
    whole_frames = whole_frames.reshape(set_count, frame_size, patch_size, series_count, width)
    whole_frames = jnp.transpose(whole_frames, (0, 2, 1, 3, 4)).reshape(
        set_count, device_count * series_count, width
    )
    flat_space, rounded_space = mix_partial(whole_frames, gain_space, qkv_space, out_space, False)
    summed_space = lax.psum(rounded_space.astype(jnp.bfloat16), "head").astype(jnp.float32)
    result = flat_space.astype(jnp.float32) + summed_space
    return result.reshape(whole_frames.shape)


F32 = jnp.float32
BF16 = jnp.bfloat16
KINDS = 3
NT = (((1,), (1,)), ((), ()))


def run(body, outs, *args, scratch=(), sems=0):
    vmem = pl.BlockSpec(memory_space=pltpu.VMEM)
    single = not isinstance(outs, list)
    shapes = [jax.ShapeDtypeStruct(*o) for o in ([outs] if single else outs)]
    found = pl.pallas_call(
        body,
        out_shape=shapes,
        in_specs=[pl.BlockSpec(memory_space=pltpu.HBM) if sems else vmem] * len(args),
        out_specs=[vmem] * len(shapes),
        scratch_shapes=[pltpu.VMEM(*s) for s in scratch]
        + [pltpu.SemaphoreType.DMA((sems,))] * (sems > 0),
        compiler_params=pltpu.CompilerParams(vmem_limit_bytes=16 << 20),
    )(*args)
    return found[0] if single else found


def lanes(value, start, size):
    return lax.slice_in_dim(value, start, start + size, axis=1)


def exchange(messages):
    count = len(messages)
    found = [messages[0]]
    for k in range(1, count):
        pairs = [(i, i ^ k) for i in range(count)]
        found.append(lax.ppermute(messages[k], "frame", pairs))
    return found


def pick_rows(value, source):
    column = lax.broadcasted_iota(jnp.int32, (source.shape[0], value.shape[0]), 1)
    chosen = jnp.where(column == source, 1.0, 0.0).astype(BF16)
    return jnp.dot(chosen, value.astype(BF16), preferred_element_type=F32)


def in_three(value):
    high = value.astype(BF16).astype(F32)
    middle = (value - high).astype(BF16).astype(F32)
    return high, middle, value - high - middle


def tail_of(items, rows, size):
    lane = lax.broadcasted_iota(jnp.int32, (rows, size), 1)
    tail = jnp.zeros((rows, size), F32)
    for at, item in enumerate(items):
        tail = jnp.where(lane == at, item, tail)
    return tail


def from_three(tail, at):
    lane = lax.broadcasted_iota(jnp.int32, tail.shape, 1)
    return jnp.sum(jnp.where((lane >= at) & (lane < at + 3), tail, 0.0), axis=-1, keepdims=True)


def rows_of(block_ref):
    return jnp.concatenate([block_ref[i].astype(F32) for i in range(block_ref.shape[0])], axis=0)


def load_body(weight_ref, held_ref, sems):
    copy = pltpu.make_async_copy(weight_ref, held_ref, sems.at[0])
    copy.start()
    copy.wait()


def slices_of(gain_ref, gains):
    for s in range(gains.shape[0]):
        row = lanes(gain_ref[...].reshape(1, -1), s * gains.shape[2], gains.shape[2])
        gains[s] = jnp.broadcast_to(row, gains.shape[1:])
    return gains[lax.axis_index("frame")]


def project_body(count, *refs):
    parts, gain_ref, weight_ref, outs = refs[:count], *refs[count : count + 2], refs[count + 2 : -2]
    tokens, total = refs[-2:]
    f = lax.axis_index("frame")
    share = tokens.shape[2]
    plane = tokens.shape[1]
    rows = plane // count
    gain = gain_ref[...].reshape(1, -1)
    for k in range(count):
        place = pl.multiple_of((f ^ k) * rows, rows)
        x = rows_of(parts[k])
        centred = x - jnp.mean(x, axis=-1, keepdims=True)
        spread = jnp.mean(centred * centred, axis=-1, keepdims=True)
        y = centred * lax.rsqrt(spread + 1e-06) * gain
        for s in range(count):
            tokens[s, pl.ds(place, rows), :] = lanes(y, s * share, share)
    row = lax.broadcasted_iota(jnp.int32, (plane, 1), 0)
    source = lax.rem(row, rows) * count + lax.div(row, rows)
    x = pick_rows(tokens[f], source).astype(BF16)
    found = [jnp.dot(x, weight_ref[t], preferred_element_type=F32) for t in range(KINDS)]
    total[...] = jnp.concatenate(found, axis=1)
    for k in range(count):
        place = pl.multiple_of((f ^ k) * rows, rows)
        outs[k][...] = total[pl.ds(place, rows), :].astype(BF16)


def prepare_body(count, *refs):
    parts, gain_ref, weight_ref = refs[:count], refs[count], refs[count + 1]
    fixed_ref, gain_own, raw_own, raw_other, gains, raw = refs[count + 2 :]
    f, p = lax.axis_index("frame"), lax.axis_index("patch")
    g = slices_of(gain_ref, gains)
    gain_own[...] = g
    g = g.astype(BF16)
    rows = [jnp.dot(g, weight_ref[t], preferred_element_type=F32) for t in range(KINDS)]
    row = lax.broadcasted_iota(jnp.int32, rows[0].shape, 0)
    fixed_ref[...] = jnp.where(row == 0, rows[0], jnp.where(row == 1, rows[1], rows[2]))
    share = gains.shape[2]
    places = parts[0].shape[1]
    rows = 2 * places
    for k in range(count):
        place = pl.multiple_of((f ^ k) * rows, rows)
        x = rows_of(parts[k])
        for s in range(count):
            raw[s, pl.ds(place, rows), :] = lanes(x, s * share, share)
    whole = raw[f]
    even, odd = (
        jnp.concatenate([whole[r + at : r + at + places] for r in range(0, count * rows, rows)], axis=0)
        for at in (0, places)
    )
    raw_own[...] = jnp.where(p == 0, even, odd).astype(BF16)
    raw_other[...] = jnp.where(p == 0, odd, even).astype(BF16)


def attend_rows(query, key, value):
    rows, width = query.shape
    heads = width // HEAD_WIDTH
    spread = heads * rows
    first = lax.broadcasted_iota(jnp.int32, (heads, rows, width), 0) * HEAD_WIDTH
    first = first.reshape(spread, width)
    lane = lax.broadcasted_iota(jnp.int32, (spread, width), 1)
    mine = (lane >= first) & (lane < first + HEAD_WIDTH)
    keys = jnp.where(mine, jnp.concatenate([key] * heads, axis=0), 0.0).astype(BF16)
    values = jnp.where(mine, jnp.concatenate([value] * heads, axis=0), 0.0).astype(BF16)
    scores = lax.dot_general(keys, query.astype(BF16), NT, preferred_element_type=F32)
    scores = (scores * (1.0 / HEAD_WIDTH**0.5)).reshape(heads, rows, rows)
    power = jnp.exp(scores - jnp.max(scores, axis=1, keepdims=True))
    weights = power / jnp.sum(power, axis=1, keepdims=True)
    weights = weights.reshape(spread, rows).T.astype(BF16)
    return jnp.dot(weights, values, preferred_element_type=F32)


def attend_time_body(count, *refs):
    parts, fixed_ref, out_ref = refs[:count], refs[count], refs[count + 1]
    total = sum(part[...].astype(F32) for part in parts).astype(BF16).astype(F32)
    columns = out_ref.shape[1]
    attended = attend_rows(*(lanes(total, t * columns, columns) for t in range(KINDS)))
    out_ref[...] = jnp.concatenate([attended, fixed_ref[...]], axis=0).astype(BF16)


def out_time_body(count, *refs):
    parts, weight_ref, raw_other = refs[:count], refs[count], refs[count + 1]
    own_ref, other_ref, alone_ref, tokens = refs[count + 2 :]
    f, p = lax.axis_index("frame"), lax.axis_index("patch")
    rows = tokens.shape[0] // count
    for k in range(count):
        place = pl.multiple_of((f ^ k) * rows, rows)
        tokens[pl.ds(place, rows), :] = parts[k][0:rows].astype(F32)
    half = tokens.shape[0] // 2
    row = lax.broadcasted_iota(jnp.int32, (tokens.shape[0], 1), 0)
    parity = jnp.where(row < half, p, 1 - p)
    row = lax.rem(row, half)
    source = lax.rem(row, count) * rows + 2 * lax.div(row, count) + parity
    x = pick_rows(tokens[...], source).astype(BF16)
    total = lax.dot_general(x, weight_ref[...], NT, preferred_element_type=F32)
    own_ref[...] = total[0:half].astype(BF16)
    other_ref[0:half] = total[half:].astype(BF16)
    alone_ref[...] = total[half:].astype(BF16)
    other_ref[half:] = raw_other[...]


def project_space_body(count, *refs):
    own, own_head, cross, cross_head, raw_own, gain_ref, weight_ref = refs[:7]
    outs, total = refs[7 : 7 + count], refs[7 + count]
    f, p = lax.axis_index("frame"), lax.axis_index("patch")
    half = own.shape[0]
    summed = own[...].astype(F32) + own_head[...].astype(F32)
    first = raw_own[...].astype(F32) + summed
    summed = cross[0:half].astype(F32) + cross_head[...].astype(F32)
    second = cross[half:].astype(F32) + summed
    low, high = jnp.where(p == 0, first, second), jnp.where(p == 0, second, first)
    places = half // count
    pieces = [v[i : i + places] for i in range(0, half, places) for v in (low, high)]
    x = jnp.concatenate(pieces, axis=0).astype(BF16).astype(F32)
    mean = jnp.mean(x, axis=-1, keepdims=True)
    centred = x - mean
    square = jnp.sum(centred * centred, axis=-1, keepdims=True)
    y = (centred * gain_ref[0:1]).astype(BF16)
    found = [jnp.dot(y, weight_ref[t], preferred_element_type=F32) for t in range(KINDS)]
    spare = total.shape[1] - KINDS * weight_ref.shape[2] - x.shape[1]
    tail = tail_of((*in_three(mean), *in_three(square)), x.shape[0], spare)
    total[...] = jnp.concatenate([*found, x, tail], axis=1)
    rows = total.shape[0] // count
    for k in range(count):
        place = pl.multiple_of((f ^ k) * rows, rows)
        outs[k][...] = total[pl.ds(place, rows), :].astype(BF16)


def attend_space_body(count, *refs):
    parts, fixed, refs = refs[:count], refs[count : 2 * count], refs[2 * count :]
    weight_ref, partial_ref, after_ref, held = refs
    f = lax.axis_index("frame")
    rows, columns = parts[0].shape[0], weight_ref.shape[1]
    share = weight_ref.shape[0] // count
    messages = [part[...].astype(F32) for part in parts]
    tails = [lanes(m, KINDS * columns + share, m.shape[1] - KINDS * columns - share) for m in messages]
    means = [from_three(t, 0) for t in tails]
    squares = [from_three(t, 3) for t in tails]
    mean = sum(means) / count
    square = sum(squares) + share * sum((m - mean) * (m - mean) for m in means)
    scale = lax.rsqrt(square / (share * count) + 1e-06)
    total = sum(messages)
    qkv = []
    for t in range(KINDS):
        value = lanes(total, t * columns, columns)
        for k in range(count):
            value = value + (means[k] - mean) * fixed[k][...].astype(F32)[rows + t : rows + t + 1]
        qkv.append((value * scale).astype(BF16).astype(F32))
    attended = attend_rows(*qkv).astype(BF16)
    for k in range(count):
        held[f ^ k] = lanes(messages[k], KINDS * columns, share)
    partial = lax.dot_general(attended, weight_ref[...], NT, preferred_element_type=F32)
    partial_ref[...] = partial.astype(BF16)
    after_ref[...] = jnp.concatenate([held[s] for s in range(count)], axis=1).astype(BF16)


def assemble_body(order, own, near, side, far, last, out_ref):
    f, p, g = lax.axis_index("frame"), lax.axis_index("patch"), lax.axis_index("groups")
    share, quarter = own.shape[0], own.shape[0] // 4
    out_ref[pl.ds(pl.multiple_of(f * share, share), share), :] = own[...]
    for at, k in enumerate(order):
        for piece, q in (
            (near, 2 * p + g),
            (side, 2 * (1 - p) + g),
            (far, 2 * p + 1 - g),
            (last, 2 * (1 - p) + 1 - g),
        ):
            place = pl.multiple_of((f ^ k) * share + q * quarter, quarter)
            out_ref[pl.ds(place, quarter), :] = piece[at * quarter : (at + 1) * quarter]


def finish_body(own, other, after, out_ref):
    out_ref[0] = after[...].astype(F32) + (own[...].astype(F32) + other[...].astype(F32))


def moving_tokens(video, gain_time, qkv_time, out_time, gain_space, qkv_space, out_space):
    count = lax.axis_size("frame")
    frames_here, patches_here, width = video.shape
    share, columns = out_time.shape
    rows = frames_here * patches_here
    plane = rows * count
    message = (KINDS * columns + share) // 128 * 128 + 128
    qkv_time, qkv_space = (jnp.transpose(w, (1, 0, 2)) for w in (qkv_time, qkv_space))
    body = functools.partial
    swap = [(0, 1), (1, 0)]

    tokens = exchange([video] * count)
    quarter = 2 * lax.axis_index("patch") + lax.axis_index("groups")
    piece = lax.dynamic_slice_in_dim(out_space, quarter * (share // 4), share // 4)
    qkv_time = run(load_body, (qkv_time.shape, BF16), qkv_time, sems=1)
    partial_time = run(
        body(project_body, count),
        [((rows, KINDS * columns), BF16)] * count,
        *tokens,
        gain_time,
        qkv_time,
        scratch=[((count, plane, share), F32), ((plane, KINDS * columns), F32)],
    )
    partial_time = exchange(partial_time)
    near, order, sides = piece, [0], []
    for stage in range(count.bit_length() - 1):
        hop = count >> (stage + 1)
        pairs = [(i, i ^ hop) for i in range(count)]
        arrived = lax.ppermute(near, "frame", pairs)
        near = jnp.concatenate([near, arrived], axis=0)
        sides.append(lax.ppermute(arrived, "patch", swap))
        order += [k ^ hop for k in order]
    near = near[share // 4 :]
    side = jnp.concatenate(sides, axis=0)
    far = []
    for value in (near, side):
        far.append(lax.ppermute(value, "groups", swap))
    whole_space = run(
        body(assemble_body, order[1:]), ((width, columns), BF16), out_space, near, side, *far
    )
    fixed, gain_own, raw_own, raw_other = run(
        body(prepare_body, count),
        [
            ((8, columns), F32),
            ((8, share), F32),
            ((plane // 2, share), BF16),
            ((plane // 2, share), BF16),
        ],
        *tokens,
        gain_space,
        qkv_space,
        scratch=[((count, 8, share), F32), ((count, plane, share), F32)],
    )
    attended = run(
        body(attend_time_body, count), ((rows + 8, columns), BF16), *partial_time, fixed
    )
    attended = exchange([attended] * count)
    own, cross, cross_only = run(
        body(out_time_body, count),
        [((plane // 2, share), BF16), ((plane, share), BF16), ((plane // 2, share), BF16)],
        *attended,
        out_time,
        raw_other,
        scratch=[((plane, columns), F32)],
    )
    own_head = lax.ppermute(own, "head", swap)
    crossed = lax.ppermute(cross, "patch", swap)
    cross_head = lax.ppermute(cross_only, ("patch", "head"), [(i, 3 - i) for i in range(4)])
    partial_space = run(
        body(project_space_body, count),
        [((rows, message), BF16)] * count,
        own,
        own_head,
        crossed,
        cross_head,
        raw_own,
        gain_own,
        qkv_space,
        scratch=[((plane, message), F32)],
    )
    partial_space = exchange(partial_space)
    mine, after = run(
        body(attend_space_body, count),
        [((rows, width), BF16)] * 2,
        *partial_space,
        *attended,
        whole_space,
        scratch=[((count, rows, share), F32)],
    )
    theirs = lax.ppermute(mine, "head", swap)
    return run(finish_body, ((1, rows, width), F32), mine, theirs, after)


def solution(mesh):
    placed = (
        P(("groups", "frame"), "patch", None),
        P(),
        P("frame", None, "head"),
        P("frame", "head"),
        P(),
        P("frame", None, "head"),
        P("frame", "head"),
    )

    def program(video, *rest):
        frames_here, patches_here, width = video.shape
        count = lax.axis_size("frame")
        small = (
            patches_here == count
            and frames_here == lax.axis_size("patch") == lax.axis_size("head") == 2
            and lax.axis_size("groups") == 2
            and frames_here * patches_here == 8
            and frames_here * count * patches_here < width
        )
        return (moving_tokens if small else on_device)(video, *rest)

    return jax.shard_map(
        program,
        mesh=mesh,
        in_specs=placed,
        out_specs=P(("groups", "frame", "patch"), None, None),
        check_vma=False,
    )
```
